256 devices in a mesh: blk: 64 (over y, x, z_lo), head: 4 (over z_hi, core).
Axes of the slice: x: 4, y: 4, z: 8 (z_hi: 2, z_lo: 4; z = z_hi * 4 + z_lo), core: 2. Of those that a mesh axis runs over, the one named last changes fastest.
Arguments:
- hidden_in: bfloat16 [32768, 2048], P('blk'), may hold values from -6 to 6
- layer_input: bfloat16 [32768, 256], P(('blk', 'head')), may hold values from -6 to 6
- in_gain: float32 [2048], replicated, may hold values from 0.5 to 1.5
- w_query: bfloat16 [2048, 2048], P(None, 'head'), may hold values from -0.125 to 0.125
- w_keyval: bfloat16 [2048, 1024], P(None, 'head'), may hold values from -0.125 to 0.125
- q_gain: float32 [256], replicated, may hold values from 0.2 to 0.45
- k_gain: float32 [256], replicated, may hold values from 0.2 to 0.45
- w_out: bfloat16 [2048, 2048], P('head'), may hold values from -0.125 to 0.125
- post_gain: float32 [2048], replicated, may hold values from 0.5 to 1.5
- laurel_left: bfloat16 [2048, 64], replicated, may hold values from -0.125 to 0.125
- laurel_right: bfloat16 [64, 2048], replicated, may hold values from -0.75 to 0.75
- laurel_gain: float32 [2048], replicated, may hold values from 0.5 to 1.5
- w_plgate: bfloat16 [2048, 256], replicated, may hold values from -0.125 to 0.125
- w_plproj: bfloat16 [256, 2048], replicated, may hold values from -0.375 to 0.375
- pl_gain: float32 [2048], replicated, may hold values from 0.5 to 1.5
- kv_pool: bfloat16 [768, 4, 128, 256], P('blk'), may hold values from -44 to 44, as said below
- page_table: int32 [64, 12], P('blk'), may hold values from 0 to 11, each once within a row
- prefix_len: int32 [64], P('blk'), may hold values from 1 to 1536, as said below
- decode_owner: int32 [64], replicated, may hold values from 0 to 63, each once
Outputs:
- mixed: bfloat16 [32768, 2048], P(('blk', 'head'))
- decode_kv: bfloat16 [4, 64, 2048, 256], P('head', 'blk')
The draws below stay inside these ranges and needn't reach their ends.
Inputs may be any that keep to these rules, and one draw needn't show every extreme that they name: `kv_pool`: cached keys and values; one request's prefix fills its 12 pages in every draw. `page_table`: each row names each of its 12 pool pages once. `prefix_len`: some request has exactly 1536 cached tokens. `decode_owner`: each request has its own slot.
All inputs are finite; a program needn't handle non-finite values.
Results may differ from the reference program's by a relative error of at most 0.009.
Values may be sent and summed in bfloat16 or wider, within the bound.
No kernel may reach another device: no remote copies, remote signals or barrier semaphores. Data moves between devices by JAX's collectives and lax.ppermute only.
A program may use at most 128 MiB of HBM per device.

```python
import math
import jax
import jax.numpy as jnp
from jax import lax

D = 2048
QH = 8
KVH = 2
HD = 256
RANK = 64
PLI = 256
NEW = 512
PAGE = 128
PAGES = 12
REQ = 64
TOKENS = 32768
POOL_PAGES = 768
N_HEAD = 4


def draw_kv_pool(key, part):
    key_normal = jax.random.fold_in(key, 0)
    pool_shape = (POOL_PAGES, 2 * KVH, PAGE, HD)
    values_raw = jnp.clip(jax.random.normal(key_normal, pool_shape, jnp.float32), -6.0, 6.0)
    is_key = (jnp.arange(2 * KVH) < KVH).reshape(1, 2 * KVH, 1, 1)
    factor = jnp.where(is_key, 0.3, 1.0)
    return (values_raw * factor).astype(jnp.bfloat16)


def draw_prefix_len(key, part):
    key_shift, key_cut, key_top = jax.random.split(key, 3)
    prefix_max = PAGES * PAGE
    shifts = jax.random.randint(key_shift, (REQ,), 0, 4)
    divisor = jnp.left_shift(jnp.ones((REQ,), jnp.int32), shifts)
    span_len = jnp.maximum(prefix_max // divisor, 1)
    cuts = jax.random.randint(key_cut, (REQ,), jnp.zeros((REQ,), jnp.int32), span_len)
    lengths = jnp.maximum(span_len - cuts, 1)
    chosen = jax.random.randint(key_top, (), 0, REQ)
    return jnp.where(jnp.arange(REQ) == chosen, prefix_max, lengths).astype(jnp.int32)


def level_of(key, dims, shards, low, top_value):
    level = 1.0
    for axis_at, shards_of in shards:
        draws = jax.random.uniform(jax.random.fold_in(jax.random.fold_in(key, 6), axis_at), (shards_of,), jnp.float32, low / len(shards), top_value / len(shards))
        level = level * jnp.repeat(jnp.exp(draws), dims[axis_at] // shards_of).reshape((-1,) + (1,) * (len(dims) - 1 - axis_at))
    return level


def centred(stream_key, extent, deviation, limit, cuts=(), kind=jnp.bfloat16):
    array = deviation * jax.random.normal(stream_key, extent, jnp.float32)
    if cuts:
        array = array * level_of(stream_key, extent, cuts, -0.22, 0.18)
    return jnp.clip(array, -limit, limit).astype(kind)


def setup_inputs(seed: int = 0) -> dict:
    keys = jax.random.split(jax.random.key(seed), 20)
    return {
        "hidden_in": centred(keys[0], (TOKENS, D), 1.0, 6.0, ((0, 64),)),
        "layer_input": centred(keys[1], (TOKENS, PLI), 1.0, 6.0, ((0, 256),)),
        "in_gain": jnp.clip(1.0 + 0.1 * jax.random.normal(keys[2], (D,), jnp.float32), 0.5, 1.5),
        "w_query": centred(keys[3], (D, QH * HD), D ** -0.5, 0.125, ((1, 4),)),
        "w_keyval": centred(keys[4], (D, 2 * KVH * HD), D ** -0.5, 0.125, ((1, 4),)),
        "q_gain": jnp.clip(jnp.exp(jax.random.uniform(keys[5], (HD,), jnp.float32, math.log(0.2), math.log(0.45))), 0.2, 0.45),
        "k_gain": jnp.clip(jnp.exp(jax.random.uniform(keys[6], (HD,), jnp.float32, math.log(0.2), math.log(0.45))), 0.2, 0.45),
        "w_out": centred(keys[7], (QH * HD, D), (QH * HD) ** -0.5, 0.125, ((0, 4),)),
        "post_gain": jnp.clip(1.0 + 0.1 * jax.random.normal(keys[8], (D,), jnp.float32), 0.5, 1.5),
        "laurel_left": centred(keys[9], (D, RANK), D ** -0.5, 0.125),
        "laurel_right": centred(keys[10], (RANK, D), RANK ** -0.5, 0.75),
        "laurel_gain": jnp.clip(1.0 + 0.1 * jax.random.normal(keys[11], (D,), jnp.float32), 0.5, 1.5),
        "w_plgate": centred(keys[12], (D, PLI), D ** -0.5, 0.125),
        "w_plproj": centred(keys[13], (PLI, D), PLI ** -0.5, 0.375),
        "pl_gain": jnp.clip(1.0 + 0.1 * jax.random.normal(keys[14], (D,), jnp.float32), 0.5, 1.5),
        "kv_pool": draw_kv_pool(jax.random.fold_in(keys[19], 71), 0),
        "page_table": jax.vmap(lambda own: jax.random.permutation(own, PAGES))(jax.random.split(keys[16], REQ)).reshape((REQ, PAGES)).astype(jnp.int32),
        "prefix_len": draw_prefix_len(jax.random.fold_in(keys[19], 71), 0),
        "decode_owner": jax.random.permutation(keys[18], REQ).astype(jnp.int32),
    }


eps = 1e-06
rope_base = 1000000.0

def rms_scale(values):
    return values * lax.rsqrt(lax.optimization_barrier(jnp.mean(values * values, axis=-1, keepdims=True)) + eps)

def rotate(values, positions):
    half_dim = values.shape[-1] // 2
    frequency = rope_base ** (-jnp.arange(half_dim, dtype=jnp.float32) / half_dim)
    angles = positions.astype(jnp.float32)[:, None] * frequency[None, :]
    cosine = jnp.cos(angles)
    sine_part = jnp.sin(angles)
    lower_half = values[..., :half_dim]
    upper_half = values[..., half_dim:]
    return jnp.concatenate([lower_half * cosine - upper_half * sine_part, upper_half * cosine + lower_half * sine_part], axis=-1)

def reference(hidden_in, layer_input, in_gain, w_query, w_keyval, q_gain, k_gain, w_out, post_gain, laurel_left, laurel_right, laurel_gain, w_plgate, w_plproj, pl_gain, kv_pool, page_table, prefix_len, decode_owner):
    prefix_max = PAGES * PAGE
    group_size = QH // KVH
    stretch_cols = QH * HD // N_HEAD

    def per_request(req_idx):
        tokens_in = lax.dynamic_slice_in_dim(hidden_in, req_idx * NEW, NEW, 0)
        plane_in = lax.dynamic_slice_in_dim(layer_input, req_idx * NEW, NEW, 0)
        length = prefix_len[req_idx]
        positions = length + jnp.arange(NEW, dtype=jnp.int32)
        normed = (rms_scale(tokens_in.astype(jnp.float32)) * in_gain).astype(jnp.bfloat16)
        queries = jnp.dot(normed, w_query, preferred_element_type=jnp.float32).reshape(NEW, QH, HD)
        queries = rotate(jnp.transpose(rms_scale(queries) * q_gain, (1, 0, 2)), positions).astype(jnp.bfloat16)
        kv_proj = rms_scale(jnp.dot(normed, w_keyval, preferred_element_type=jnp.float32).reshape(NEW, 2 * KVH, HD))
        kv_proj = jnp.transpose(kv_proj, (1, 0, 2))
        key_new = rotate(kv_proj[:KVH] * k_gain, positions)
        fresh = jnp.concatenate([key_new, kv_proj[KVH:]], axis=0).astype(jnp.bfloat16)
        pool_rows = lax.dynamic_slice_in_dim(kv_pool, req_idx * PAGES, PAGES, 0)
        table_row = page_table[req_idx]
        my_pages = jnp.take(pool_rows, table_row, axis=0)
        old_all = jnp.transpose(my_pages, (1, 0, 2, 3)).reshape(2 * KVH, prefix_max, HD)
        live_mask = jnp.arange(prefix_max, dtype=jnp.int32) < length
        old_all = jnp.where(live_mask[None, :, None], old_all, jnp.zeros_like(old_all))
        keys_all = jnp.concatenate([old_all[:KVH], fresh[:KVH]], axis=1).astype(jnp.float32)
        vals_all = jnp.concatenate([old_all[KVH:], fresh[KVH:]], axis=1).astype(jnp.float32)
        grouped_q = queries.reshape(KVH, group_size * NEW, HD).astype(jnp.float32)
        scores = jnp.einsum('gqd,gkd->gqk', grouped_q, keys_all)
        row_pos = jnp.tile(jnp.arange(NEW, dtype=jnp.int32), group_size)
        key_idx = jnp.arange(prefix_max + NEW, dtype=jnp.int32)
        allowed_old = (key_idx[None, :] < prefix_max) & (key_idx[None, :] < length)
        allowed_new = (key_idx[None, :] >= prefix_max) & (key_idx[None, :] - prefix_max <= row_pos[:, None])
        allowed = allowed_old | allowed_new
        scores = jnp.where(allowed[None], scores, -jnp.inf)
        row_top = lax.optimization_barrier(jnp.max(scores, axis=-1, keepdims=True))
        expo = jnp.exp(scores - row_top)
        row_total = lax.optimization_barrier(jnp.sum(expo, axis=-1, keepdims=True))
        weights = expo.astype(jnp.bfloat16)
        attn = jnp.einsum('gqk,gkd->gqd', weights.astype(jnp.float32), vals_all) / row_total
        attn = attn.astype(jnp.bfloat16).reshape(QH, NEW, HD)
        attn = jnp.transpose(attn, (1, 0, 2)).reshape(NEW, QH * HD)
        parts = jnp.einsum('tgc,gcd->gtd', attn.reshape(NEW, N_HEAD, stretch_cols).astype(jnp.float32), w_out.reshape(N_HEAD, stretch_cols, D).astype(jnp.float32))
        proj = lax.optimization_barrier(jnp.sum(parts.astype(jnp.bfloat16).astype(jnp.float32), axis=0))
        branch_low = jnp.dot(normed, laurel_left, preferred_element_type=jnp.float32).astype(jnp.bfloat16)
        laurel = normed.astype(jnp.float32) + rms_scale(jnp.dot(branch_low, laurel_right, preferred_element_type=jnp.float32)) * laurel_gain
        state = (tokens_in.astype(jnp.float32) + rms_scale(proj) * post_gain + laurel) * 2.0 ** (-0.5)
        state_b = state.astype(jnp.bfloat16)
        gated = (jax.nn.gelu(jnp.dot(state_b, w_plgate, preferred_element_type=jnp.float32), approximate=True) * plane_in.astype(jnp.float32)).astype(jnp.bfloat16)
        mixed_rows = (state + rms_scale(jnp.dot(gated, w_plproj, preferred_element_type=jnp.float32)) * pl_gain).astype(jnp.bfloat16)
        base_seq = jnp.concatenate([old_all, jnp.zeros((2 * KVH, NEW, HD), jnp.bfloat16)], axis=1)
        full_seq = lax.dynamic_update_slice(base_seq, fresh, (jnp.int32(0), length.astype(jnp.int32), jnp.int32(0)))
        return (mixed_rows, full_seq)
    mixed_all, seq_all = lax.map(per_request, jnp.arange(REQ, dtype=jnp.int32))
    mixed = mixed_all.reshape(REQ * NEW, D)
    inverse = jnp.zeros((REQ,), jnp.int32).at[decode_owner.astype(jnp.int32)].set(jnp.arange(REQ, dtype=jnp.int32))
    arranged = jnp.take(seq_all, inverse, axis=0)
    decode_kv = jnp.transpose(arranged, (1, 0, 2, 3))
    return (mixed, decode_kv)
```

```python
import functools

import jax
import jax.numpy as jnp
from jax import lax
from jax.experimental import pallas as pl
from jax.experimental.pallas import tpu as pltpu
from jax.sharding import PartitionSpec as P

QH = 8
KVH = 2
eps = 1e-06
rope_base = 1000000.0
F32 = jnp.float32
BF16 = jnp.bfloat16
ANY = pl.ANY
AXES = ("blk", "head")


def rms_scale(values):
    return values * lax.rsqrt(jnp.mean(values * values, axis=-1, keepdims=True) + eps)


def turn(values, cosine, sine):
    half = values.shape[-1] // 2
    low, high = values[:, :half], values[:, half:]
    return jnp.concatenate([low * cosine - high * sine, high * cosine + low * sine], axis=-1)


def dot(a, b):
    return jnp.dot(a, b, preferred_element_type=F32)


def dot_t(a, b):
    return lax.dot_general(a, b, (((1,), (1,)), ((), ())), preferred_element_type=F32)


def prep_kernel(
    meta, hidden, in_gain, w_kv, k_gain, cosine, sine, pool,
    normed, fresh, seq, fresh_all, old, sem, *, n_pages, page, rows, kv_heads,
):
    step = pl.program_id(0)
    head = meta[n_pages + 1]
    length = meta[n_pages]

    def page_copy(p):
        return pltpu.make_async_copy(
            pool.at[meta[p], head], old.at[pl.ds(p * page, page)], sem.at[p]
        )

    @pl.when(step == 0)
    def _():
        for p in range(n_pages):
            page_copy(p).start()

    tile = hidden.shape[0]
    values = (rms_scale(hidden[...].astype(F32)) * in_gain[...]).astype(BF16)
    normed[...] = values
    own = rms_scale(dot(values, w_kv[...]))
    key = turn(own * k_gain[...], cosine[...], sine[...])
    slot = jnp.where(head < kv_heads, key, own).astype(BF16)
    fresh[...] = slot
    fresh_all[pl.ds(pl.multiple_of(step * tile, tile), tile), :] = slot

    @pl.when(step == pl.num_programs(0) - 1)
    def _():
        total = seq.shape[0]
        span = rows + page
        prefix = n_pages * page
        for p in range(n_pages):
            page_copy(p).wait()
        for p in range(n_pages):
            at = p * page + lax.broadcasted_iota(jnp.int32, (page, 1), 0)
            part = old[p * page : (p + 1) * page, :].astype(F32)
            seq[p * page : (p + 1) * page, :] = jnp.where(at < length, part, 0.0).astype(BF16)
        seq[prefix:total, :] = jnp.zeros((total - prefix, seq.shape[1]), BF16)
        base = jnp.minimum(length // page * page, total - span)
        base = pl.multiple_of(base, page)
        row = base + lax.broadcasted_iota(jnp.int32, (span, 1), 0)
        col = lax.broadcasted_iota(jnp.int32, (span, rows), 1)
        pick = jnp.where(row - length == col, 1.0, 0.0).astype(BF16)
        placed = dot(pick, fresh_all[...])
        window = seq[pl.ds(base, span), :].astype(F32)
        seq[pl.ds(base, span), :] = jnp.where(row < length, window, placed).astype(BF16)


def query_kernel(normed, w_q, q_gain, cosine, sine, queries):
    heads, _, dim = queries.shape
    raw = dot(normed[...], w_q[...])
    for h in range(heads):
        part = rms_scale(raw[:, h * dim : (h + 1) * dim]) * q_gain[...]
        queries[h] = turn(part, cosine[...], sine[...]).astype(BF16)


def attend_kernel(
    meta, queries, w_out, pool, fresh, via_chip, via_core, via_both,
    send, mine, keys, vals, sem, *, n_pages, page, kv_heads, group,
):
    step = pl.program_id(0)
    head = meta[n_pages + 1]
    length = meta[n_pages]
    heads, tile, dim = queries.shape
    kv_of = head * heads // group
    prefix = n_pages * page
    rows = fresh.shape[0]

    @pl.when(step == 0)
    def _():
        copies = []
        for p in range(n_pages):
            for i, buf, slot in ((0, keys, kv_of), (1, vals, kv_of + kv_heads)):
                copies.append(
                    pltpu.make_async_copy(
                        pool.at[meta[p], slot], buf.at[pl.ds(p * page, page)], sem.at[i, p]
                    )
                )
        for copy in copies:
            copy.start()
        sources = (
            (fresh, via_chip),
            (via_core, via_both),
            (via_both, via_core),
            (via_chip, fresh),
        )
        for h, (key_src, val_src) in enumerate(sources):

            @pl.when(head == h)
            def _():
                new_key = pltpu.make_async_copy(
                    key_src, keys.at[pl.ds(prefix, rows)], sem.at[0, n_pages]
                )
                new_val = pltpu.make_async_copy(
                    val_src, vals.at[pl.ds(prefix, rows)], sem.at[1, n_pages]
                )
                new_key.start()
                new_val.start()
                new_key.wait()
                new_val.wait()

        for copy in copies:
            copy.wait()

    quarter = tile_of(step, head)
    flat = queries[...].reshape(heads * tile, dim)
    scores = dot_t(flat, keys[...])
    col = lax.broadcasted_iota(jnp.int32, (1, prefix + rows), 1)
    row = lax.broadcasted_iota(jnp.int32, (heads * tile, 1), 0)
    token = quarter * tile + jnp.where(row >= tile, row - tile, row)
    lowest = jnp.where(col < prefix, jnp.where(col < length, -1, rows), col - prefix)
    scores = jnp.where(lowest <= token, scores, -jnp.inf)
    top = jnp.max(scores, axis=1, keepdims=True)
    expo = jnp.exp(scores - top)
    total = jnp.sum(expo, axis=1, keepdims=True)
    attn = (dot(expo.astype(BF16), vals[...]) / total).astype(BF16)
    part = dot(attn[:tile], w_out[:dim, :])
    for h in range(1, heads):
        part = part + dot(attn[h * tile : (h + 1) * tile], w_out[h * dim : (h + 1) * dim, :])
    part = part.astype(BF16)

    @pl.when(step < 2)
    def _():
        send[0] = part

    @pl.when(step >= 2)
    def _():
        mine[0] = part


def tile_of(step, head):
    core = head % 2
    chip = head // 2
    to_core = jnp.where(step < 2, 1 - core, core)
    to_chip = jnp.where(step % 2 == 0, 1 - chip, chip)
    return to_chip * 2 + to_core


def post_kernel(
    meta, hidden, normed, mine, partner, far, plane, post_gain, left, right, laurel_gain,
    gate, proj, pl_gain, mixed,
):
    total = mine[0].astype(F32) + partner[0].astype(F32) + far[...].astype(F32)
    low = dot_t(normed[...], left[...]).astype(BF16)
    laurel = normed[...].astype(F32) + rms_scale(dot(low, right[...])) * laurel_gain[...]
    state = (hidden[...].astype(F32) + rms_scale(total) * post_gain[...] + laurel) * 2.0 ** (-0.5)
    gated = jax.nn.gelu(dot(state.astype(BF16), gate[...]), approximate=True)
    gated = (gated * plane[...].astype(F32)).astype(BF16)
    mixed[...] = (state + rms_scale(dot(gated, proj[...])) * pl_gain[...]).astype(BF16)


def permute_kernel(owner, spread, after, arranged, sem):
    count = spread.shape[0]

    def send(r, carry):
        pltpu.make_async_copy(spread.at[r], arranged.at[owner[r]], sem).start()
        return carry

    lax.fori_loop(0, count, send, 0)
    pltpu.make_async_copy(spread, arranged, sem).wait()


def whole(shape):
    zeros = (0,) * len(shape)
    return pl.BlockSpec(shape, lambda *_: zeros)


def on_device(
    hidden_in, layer_input, in_gain, w_query, w_keyval, q_gain, k_gain, w_out, post_gain,
    laurel_left, laurel_right, laurel_gain, w_plgate, w_plproj, pl_gain, kv_pool, page_table,
    prefix_len, decode_owner,
):
    rows, width = hidden_in.shape
    dim = kv_pool.shape[3]
    page = kv_pool.shape[2]
    n_pages = page_table.shape[1]
    kv_heads = kv_pool.shape[1] // 2
    heads = w_query.shape[1] // dim
    prefix = n_pages * page
    total_len = prefix + rows
    blocks = lax.axis_size("blk")
    group = QH // KVH
    n_head = lax.axis_size("head")
    quarter = rows // n_head
    head = lax.axis_index("head").astype(jnp.int32)
    meta = jnp.concatenate([page_table[0], prefix_len, head[None]])

    half = dim // 2
    frequency = rope_base ** (-jnp.arange(half, dtype=F32) / half)
    positions = prefix_len[0] + jnp.arange(rows, dtype=jnp.int32)
    angles = positions.astype(F32)[:, None] * frequency[None, :]
    cosine, sine = jnp.cos(angles), jnp.sin(angles)

    in_gain, q_gain, k_gain = in_gain[None], q_gain[None], k_gain[None]
    post_gain, laurel_gain, pl_gain = post_gain[None], laurel_gain[None], pl_gain[None]

    tile = quarter
    steps = rows // tile
    normed, fresh, full_seq = pl.pallas_call(
        functools.partial(
            prep_kernel, n_pages=n_pages, page=page, rows=rows, kv_heads=kv_heads
        ),
        grid_spec=pltpu.PrefetchScalarGridSpec(
            num_scalar_prefetch=1,
            grid=(steps,),
            in_specs=[
                pl.BlockSpec((tile, width), lambda i, m: (i, 0)),
                whole((1, width)),
                whole((width, dim)),
                whole((1, dim)),
                pl.BlockSpec((tile, half), lambda i, m: (i, 0)),
                pl.BlockSpec((tile, half), lambda i, m: (i, 0)),
                pl.BlockSpec(memory_space=ANY),
            ],
            out_specs=[
                pl.BlockSpec((tile, width), lambda i, m: (i, 0)),
                pl.BlockSpec((tile, dim), lambda i, m: (i, 0)),
                whole((total_len, dim)),
            ],
            scratch_shapes=[
                pltpu.VMEM((rows, dim), BF16),
                pltpu.VMEM((prefix, dim), BF16),
                pltpu.SemaphoreType.DMA((n_pages,)),
            ],
        ),
        out_shape=[
            jax.ShapeDtypeStruct((rows, width), BF16),
            jax.ShapeDtypeStruct((rows, dim), BF16),
            jax.ShapeDtypeStruct((total_len, dim), BF16),
        ],
        name="prep",
    )(meta, hidden_in, in_gain, w_keyval, k_gain, cosine, sine, kv_pool)

    def pairs(moves):
        return [(b * n_head + s, b * n_head + t) for b in range(blocks) for s, t in moves]

    via_chip = lax.ppermute(fresh, AXES, pairs(((1, 3), (2, 0))))
    via_core = lax.ppermute(fresh, AXES, pairs(((0, 1), (3, 2))))
    via_both = lax.ppermute(via_chip, AXES, pairs(((0, 1), (3, 2))))
    spread = lax.all_to_all(
        full_seq.reshape(blocks, total_len // blocks, dim), "blk", 0, 0, tiled=True
    )

    queries = pl.pallas_call(
        query_kernel,
        grid=(steps,),
        in_specs=[
            pl.BlockSpec((tile, width), lambda i: (i, 0)),
            whole(w_query.shape),
            whole((1, dim)),
            pl.BlockSpec((tile, half), lambda i: (i, 0)),
            pl.BlockSpec((tile, half), lambda i: (i, 0)),
        ],
        out_specs=pl.BlockSpec((heads, tile, dim), lambda i: (0, i, 0)),
        out_shape=jax.ShapeDtypeStruct((heads, rows, dim), BF16),
        name="query",
    )(normed, w_query, q_gain, cosine, sine)

    send, mine = pl.pallas_call(
        functools.partial(
            attend_kernel, n_pages=n_pages, page=page, kv_heads=kv_heads, group=group
        ),
        grid_spec=pltpu.PrefetchScalarGridSpec(
            num_scalar_prefetch=1,
            grid=(n_head,),
            in_specs=[
                pl.BlockSpec(
                    (heads, quarter, dim), lambda i, m: (0, tile_of(i, m[n_pages + 1]), 0)
                ),
                whole(w_out.shape),
            ]
            + [pl.BlockSpec(memory_space=ANY)] * 5,
            out_specs=[
                pl.BlockSpec((1, quarter, width), lambda i, m: (jnp.minimum(i, 1), 0, 0)),
                pl.BlockSpec((1, quarter, width), lambda i, m: (jnp.maximum(i - 2, 0), 0, 0)),
            ],
            scratch_shapes=[
                pltpu.VMEM((total_len, dim), BF16),
                pltpu.VMEM((total_len, dim), BF16),
                pltpu.SemaphoreType.DMA((2, n_pages + 1)),
            ],
        ),
        out_shape=[jax.ShapeDtypeStruct((2, quarter, width), BF16)] * 2,
        name="attend",
    )(meta, queries, w_out, kv_pool, fresh, via_chip, via_core, via_both)

    core_pairs = pairs(((0, 1), (1, 0), (2, 3), (3, 2)))
    chip_pairs = pairs(((0, 2), (1, 3), (2, 0), (3, 1)))
    partner = lax.ppermute(send, AXES, core_pairs)
    pair_sum = (mine[0].astype(F32) + partner[0].astype(F32)).astype(BF16)
    far = lax.ppermute(pair_sum, AXES, chip_pairs)

    mixed = pl.pallas_call(
        post_kernel,
        grid_spec=pltpu.PrefetchScalarGridSpec(
            num_scalar_prefetch=1,
            grid=(1,),
            in_specs=[
                pl.BlockSpec((quarter, width), lambda i, m: (m[n_pages + 1], 0)),
                pl.BlockSpec((quarter, width), lambda i, m: (m[n_pages + 1], 0)),
                pl.BlockSpec((1, quarter, width), lambda i, m: (1, 0, 0)),
                pl.BlockSpec((1, quarter, width), lambda i, m: (1, 0, 0)),
                whole((quarter, width)),
                whole(layer_input.shape),
                whole((1, width)),
                whole(laurel_left.shape[::-1]),
                whole(laurel_right.shape),
                whole((1, width)),
                whole(w_plgate.shape),
                whole(w_plproj.shape),
                whole((1, width)),
            ],
            out_specs=whole((quarter, width)),
        ),
        out_shape=jax.ShapeDtypeStruct((quarter, width), BF16),
        name="post",
    )(
        meta, hidden_in, normed, mine, partner, far, layer_input, post_gain, laurel_left.T,
        laurel_right, laurel_gain, w_plgate, w_plproj, pl_gain,
    )

    arranged = pl.pallas_call(
        permute_kernel,
        grid_spec=pltpu.PrefetchScalarGridSpec(
            num_scalar_prefetch=1,
            grid=(1,),
            in_specs=[pl.BlockSpec(memory_space=ANY)] * 2,
            out_specs=pl.BlockSpec(memory_space=ANY),
            scratch_shapes=[pltpu.SemaphoreType.DMA],
        ),
        out_shape=jax.ShapeDtypeStruct(spread.shape, spread.dtype),
        name="permute",
    )(decode_owner, spread, pair_sum)
    owned = lax.all_to_all(arranged, "blk", 0, 0, tiled=True)
    return mixed, owned.reshape(1, 1, total_len, dim)


def solution(mesh):
    in_specs = (
        P("blk", None),
        P(("blk", "head"), None),
        P(),
        P(None, "head"),
        P(None, "head"),
        P(),
        P(),
        P("head", None),
        P(),
        P(),
        P(),
        P(),
        P(),
        P(),
        P(),
        P("blk", None, None, None),
        P("blk", None),
        P("blk"),
        P(),
    )
    out_specs = (P(("blk", "head"), None), P("head", "blk", None, None))
    return jax.shard_map(
        on_device, mesh=mesh, in_specs=in_specs, out_specs=out_specs, check_vma=False
    )
```

```python
import functools

import jax
import jax.numpy as jnp
from jax import lax
from jax.experimental import pallas as pl
from jax.experimental.pallas import tpu as pltpu
from jax.sharding import PartitionSpec as P

QH = 8
KVH = 2
eps = 1e-06
rope_base = 1000000.0
F32 = jnp.float32
BF16 = jnp.bfloat16
ANY = pl.ANY
AXES = ("blk", "head")


def rms_scale(values):
    return values * lax.rsqrt(jnp.mean(values * values, axis=-1, keepdims=True) + eps)


def turn(values, cosine, sine):
    half = values.shape[-1] // 2
    low, high = values[:, :half], values[:, half:]
    return jnp.concatenate([low * cosine - high * sine, high * cosine + low * sine], axis=-1)


def dot(a, b):
    return jnp.dot(a, b, preferred_element_type=F32)


def dot_t(a, b):
    return lax.dot_general(a, b, (((1,), (1,)), ((), ())), preferred_element_type=F32)


def prep_kernel(
    table, prefix_len, head_at, hidden, in_gain, w_kv, k_gain, frequency, pool,
    normed, fresh, seq, cosine, sine, fresh_all, old, sem, *, n_pages, page, rows, kv_heads,
):
    step = pl.program_id(0)
    steps = pl.num_programs(0)
    head = head_at[0]
    length = prefix_len[0]
    tile = hidden.shape[0]
    total = seq.shape[0]
    prefix = n_pages * page

    def page_copy(p):
        return pltpu.make_async_copy(
            pool.at[table[p], head], old.at[pl.ds(p * page, page)], sem.at[p]
        )

    @pl.when(step == 0)
    def _():
        for p in range(n_pages):
            page_copy(p).start()

    values = (rms_scale(hidden[...].astype(F32)) * in_gain[...]).astype(BF16)
    normed[...] = values
    own = rms_scale(dot(values, w_kv[...]))
    position = length + step * tile + lax.broadcasted_iota(jnp.int32, (tile, 1), 0)
    angles = position.astype(F32) * frequency[...]
    cos, sin = jnp.cos(angles), jnp.sin(angles)
    cosine[...] = cos
    sine[...] = sin
    key = turn(own * k_gain[...], cos, sin)
    slot = jnp.where(head < kv_heads, key, own).astype(BF16)
    fresh[...] = slot
    fresh_all[pl.ds(pl.multiple_of(step * tile, tile), tile), :] = slot

    @pl.when(step == 0)
    def _():
        for p in range(n_pages):
            page_copy(p).wait()
        for p in range(n_pages):
            at = p * page + lax.broadcasted_iota(jnp.int32, (page, 1), 0)
            part = old[p * page : (p + 1) * page, :].astype(F32)
            seq[p * page : (p + 1) * page, :] = jnp.where(at < length, part, 0.0).astype(BF16)
        seq[prefix:total, :] = jnp.zeros((total - prefix, seq.shape[1]), BF16)

    @pl.when(step == steps - 1)
    def _():
        span = rows + page
        base = jnp.minimum(length // page * page, total - span)
        base = pl.multiple_of(base, page)
        row = base + lax.broadcasted_iota(jnp.int32, (span, 1), 0)
        col = lax.broadcasted_iota(jnp.int32, (span, rows), 1)
        pick = jnp.where(row - length == col, 1.0, 0.0).astype(BF16)
        placed = dot(pick, fresh_all[...])
        window = seq[pl.ds(base, span), :].astype(F32)
        seq[pl.ds(base, span), :] = jnp.where(row < length, window, placed).astype(BF16)


def query_kernel(normed, w_q, q_gain, cosine, sine, queries):
    part = rms_scale(dot(normed[...], w_q[...])) * q_gain[...]
    queries[0] = turn(part, cosine[...], sine[...]).astype(BF16)


def attend_kernel(
    table, prefix_len, head_at, near_q, far_q, w_out, pool, fresh, via_chip, via_core, via_both,
    send, mine, keys, vals, sem, *, n_pages, page, kv_heads, group,
):
    step = pl.program_id(0)
    head = head_at[0]
    length = prefix_len[0]
    heads, tile, _ = near_q.shape
    kv_of = head * heads // group
    prefix = n_pages * page
    rows = fresh.shape[0]

    @pl.when(step == 0)
    def _():
        copies = []
        for p in range(n_pages):
            for i, buf, slot in ((0, keys, kv_of), (1, vals, kv_of + kv_heads)):
                copies.append(
                    pltpu.make_async_copy(
                        pool.at[table[p], slot], buf.at[pl.ds(p * page, page)], sem.at[i, p]
                    )
                )
        for copy in copies:
            copy.start()
        sources = (
            (fresh, via_chip),
            (via_core, via_both),
            (via_both, via_core),
            (via_chip, fresh),
        )
        for h, (key_src, val_src) in enumerate(sources):

            @pl.when(head == h)
            def _():
                new_key = pltpu.make_async_copy(
                    key_src, keys.at[pl.ds(prefix, rows)], sem.at[0, n_pages]
                )
                new_val = pltpu.make_async_copy(
                    val_src, vals.at[pl.ds(prefix, rows)], sem.at[1, n_pages]
                )
                new_key.start()
                new_val.start()
                new_key.wait()
                new_val.wait()

        for copy in copies:
            copy.wait()

    col = lax.broadcasted_iota(jnp.int32, (1, prefix + rows), 1)
    lowest = jnp.where(col < prefix, jnp.where(col < length, -1, rows), col - prefix)
    row = lax.broadcasted_iota(jnp.int32, (tile, 1), 0)
    attns = [[], []]
    for h in range(heads):
        both = jnp.concatenate([far_q[h], near_q[h]], axis=0)
        token = jnp.concatenate(
            [quarter_of(step, i, head) * tile + row for i in range(2)], axis=0
        )
        scores = jnp.where(lowest <= token, dot_t(both, keys[...]), -jnp.inf)
        top = jnp.max(scores, axis=1, keepdims=True)
        expo = jnp.exp(scores - top)
        total = jnp.sum(expo, axis=1, keepdims=True)
        attns[h] = (dot(expo.astype(BF16), vals[...]) / total).astype(BF16)
    part = dot(jnp.concatenate(attns, axis=1), w_out[...]).astype(BF16)

    @pl.when(step == 0)
    def _():
        send[0] = part[:tile]
        send[1] = part[tile:]

    @pl.when(step == 1)
    def _():
        mine[0] = part[:tile]
        mine[1] = part[tile:]


def quarter_of(step, own_chip, head):
    core = head % 2
    chip = head // 2
    to_core = jnp.where(step == 0, 1 - core, core)
    to_chip = chip if own_chip else 1 - chip
    return to_chip * 2 + to_core


def post_kernel(
    head_at, hidden, normed, mine, partner, far, plane, post_gain, left, right, laurel_gain,
    gate, proj, pl_gain, mixed,
):
    total = mine[0].astype(F32) + partner[0].astype(F32) + far[...].astype(F32)
    low = dot_t(normed[...], left[...]).astype(BF16)
    laurel = normed[...].astype(F32) + rms_scale(dot(low, right[...])) * laurel_gain[...]
    state = (hidden[...].astype(F32) + rms_scale(total) * post_gain[...] + laurel) * 2.0 ** (-0.5)
    gated = jax.nn.gelu(dot(state.astype(BF16), gate[...]), approximate=True)
    gated = (gated * plane[...].astype(F32)).astype(BF16)
    mixed[...] = (state + rms_scale(dot(gated, proj[...])) * pl_gain[...]).astype(BF16)


def permute_kernel(owner, spread, after, arranged):
    def place(r, carry):
        arranged[owner[r]] = spread[r]
        return carry

    lax.fori_loop(0, spread.shape[0], place, 0, unroll=8)


def whole(shape):
    zeros = (0,) * len(shape)
    return pl.BlockSpec(shape, lambda *_: zeros)


def on_device(
    hidden_in, layer_input, in_gain, w_query, w_keyval, q_gain, k_gain, w_out, post_gain,
    laurel_left, laurel_right, laurel_gain, w_plgate, w_plproj, pl_gain, kv_pool, page_table,
    prefix_len, decode_owner,
):
    rows, width = hidden_in.shape
    dim = kv_pool.shape[3]
    page = kv_pool.shape[2]
    n_pages = page_table.shape[1]
    kv_heads = kv_pool.shape[1] // 2
    heads = w_query.shape[1] // dim
    prefix = n_pages * page
    total_len = prefix + rows
    blocks = lax.axis_size("blk")
    group = QH // KVH
    n_head = lax.axis_size("head")
    quarter = rows // n_head
    head = lax.axis_index("head").astype(jnp.int32)
    half = dim // 2
    frequency = (rope_base ** (-jnp.arange(half, dtype=F32) / half))[None]
    scalars = (page_table[0], prefix_len, head[None])

    in_gain, q_gain, k_gain = in_gain[None], q_gain[None], k_gain[None]
    post_gain, laurel_gain, pl_gain = post_gain[None], laurel_gain[None], pl_gain[None]

    tile = rows // 2
    normed, fresh, full_seq, cosine, sine = pl.pallas_call(
        functools.partial(
            prep_kernel, n_pages=n_pages, page=page, rows=rows, kv_heads=kv_heads
        ),
        grid_spec=pltpu.PrefetchScalarGridSpec(
            num_scalar_prefetch=3,
            grid=(rows // tile,),
            in_specs=[
                pl.BlockSpec((tile, width), lambda i, *_: (i, 0)),
                whole((1, width)),
                whole((width, dim)),
                whole((1, dim)),
                whole((1, half)),
                pl.BlockSpec(memory_space=ANY),
            ],
            out_specs=[
                pl.BlockSpec((tile, width), lambda i, *_: (i, 0)),
                pl.BlockSpec((tile, dim), lambda i, *_: (i, 0)),
                whole((total_len, dim)),
                pl.BlockSpec((tile, half), lambda i, *_: (i, 0)),
                pl.BlockSpec((tile, half), lambda i, *_: (i, 0)),
            ],
            scratch_shapes=[
                pltpu.VMEM((rows, dim), BF16),
                pltpu.VMEM((prefix, dim), BF16),
                pltpu.SemaphoreType.DMA((n_pages,)),
            ],
        ),
        out_shape=[
            jax.ShapeDtypeStruct((rows, width), BF16),
            jax.ShapeDtypeStruct((rows, dim), BF16),
            jax.ShapeDtypeStruct((total_len, dim), BF16),
            jax.ShapeDtypeStruct((rows, half), F32),
            jax.ShapeDtypeStruct((rows, half), F32),
        ],
        name="prep",
    )(*scalars, hidden_in, in_gain, w_keyval, k_gain, frequency, kv_pool)

    def pairs(moves):
        return [(b * n_head + s, b * n_head + t) for b in range(blocks) for s, t in moves]

    via_chip = lax.ppermute(fresh, AXES, pairs(((1, 3), (2, 0))))
    via_core = lax.ppermute(fresh, AXES, pairs(((0, 1), (3, 2))))
    via_both = lax.ppermute(via_chip, AXES, pairs(((0, 1), (3, 2))))
    spread = lax.all_to_all(
        full_seq.reshape(blocks, total_len // blocks, dim), "blk", 0, 0, tiled=True
    )

    queries = pl.pallas_call(
        query_kernel,
        grid=(heads,),
        in_specs=[
            whole((rows, width)),
            pl.BlockSpec((width, dim), lambda i: (0, i)),
            whole((1, dim)),
            whole((rows, half)),
            whole((rows, half)),
        ],
        out_specs=pl.BlockSpec((1, rows, dim), lambda i: (i, 0, 0)),
        out_shape=jax.ShapeDtypeStruct((heads, rows, dim), BF16),
        name="query",
    )(normed, w_query, q_gain, cosine, sine)

    send, mine = pl.pallas_call(
        functools.partial(
            attend_kernel, n_pages=n_pages, page=page, kv_heads=kv_heads, group=group
        ),
        grid_spec=pltpu.PrefetchScalarGridSpec(
            num_scalar_prefetch=3,
            grid=(2,),
            in_specs=[
                pl.BlockSpec(
                    (heads, quarter, dim), lambda i, t, n, h: (0, quarter_of(i, 1, h[0]), 0)
                ),
                pl.BlockSpec(
                    (heads, quarter, dim), lambda i, t, n, h: (0, quarter_of(i, 0, h[0]), 0)
                ),
                whole(w_out.shape),
            ]
            + [pl.BlockSpec(memory_space=ANY)] * 5,
            out_specs=[whole((2, quarter, width))] * 2,
            scratch_shapes=[
                pltpu.VMEM((total_len, dim), BF16),
                pltpu.VMEM((total_len, dim), BF16),
                pltpu.SemaphoreType.DMA((2, n_pages + 1)),
            ],
        ),
        out_shape=[jax.ShapeDtypeStruct((2, quarter, width), BF16)] * 2,
        name="attend",
    )(*scalars, queries, queries, w_out, kv_pool, fresh, via_chip, via_core, via_both)

    core_pairs = pairs(((0, 1), (1, 0), (2, 3), (3, 2)))
    chip_pairs = pairs(((0, 2), (1, 3), (2, 0), (3, 1)))
    partner = lax.ppermute(send, AXES, core_pairs)
    pair_sum = (mine[0].astype(F32) + partner[0].astype(F32)).astype(BF16)
    far = lax.ppermute(pair_sum, AXES, chip_pairs)

    mixed = pl.pallas_call(
        post_kernel,
        grid_spec=pltpu.PrefetchScalarGridSpec(
            num_scalar_prefetch=1,
            grid=(1,),
            in_specs=[
                pl.BlockSpec((quarter, width), lambda i, h: (h[0], 0)),
                pl.BlockSpec((quarter, width), lambda i, h: (h[0], 0)),
                pl.BlockSpec((1, quarter, width), lambda i, h: (1, 0, 0)),
                pl.BlockSpec((1, quarter, width), lambda i, h: (1, 0, 0)),
                whole((quarter, width)),
                whole(layer_input.shape),
                whole((1, width)),
                whole(laurel_left.shape[::-1]),
                whole(laurel_right.shape),
                whole((1, width)),
                whole(w_plgate.shape),
                whole(w_plproj.shape),
                whole((1, width)),
            ],
            out_specs=whole((quarter, width)),
        ),
        out_shape=jax.ShapeDtypeStruct((quarter, width), BF16),
        name="post",
    )(
        scalars[2], hidden_in, normed, mine, partner, far, layer_input, post_gain, laurel_left.T,
        laurel_right, laurel_gain, w_plgate, w_plproj, pl_gain,
    )

    arranged = pl.pallas_call(
        permute_kernel,
        grid_spec=pltpu.PrefetchScalarGridSpec(
            num_scalar_prefetch=1,
            grid=(1,),
            in_specs=[whole(spread.shape), pl.BlockSpec(memory_space=ANY)],
            out_specs=whole(spread.shape),
        ),
        out_shape=jax.ShapeDtypeStruct(spread.shape, spread.dtype),
        name="permute",
    )(decode_owner, spread, pair_sum)
    owned = lax.all_to_all(arranged, "blk", 0, 0, tiled=True)
    return mixed, owned.reshape(1, 1, total_len, dim)


def solution(mesh):
    in_specs = (
        P("blk", None),
        P(("blk", "head"), None),
        P(),
        P(None, "head"),
        P(None, "head"),
        P(),
        P(),
        P("head", None),
        P(),
        P(),
        P(),
        P(),
        P(),
        P(),
        P(),
        P("blk", None, None, None),
        P("blk", None),
        P("blk"),
        P(),
    )
    out_specs = (P(("blk", "head"), None), P("head", "blk", None, None))
    return jax.shard_map(
        on_device, mesh=mesh, in_specs=in_specs, out_specs=out_specs, check_vma=False
    )
```

```python
import functools

import jax
import jax.numpy as jnp
from jax import lax
from jax.experimental import pallas as pl
from jax.experimental.pallas import tpu as pltpu
from jax.sharding import PartitionSpec as P

QH = 8
KVH = 2
eps = 1e-06
rope_base = 1000000.0
F32 = jnp.float32
BF16 = jnp.bfloat16
ANY = pl.ANY
AXES = ("blk", "head")


def rms_scale(values):
    return values * lax.rsqrt(jnp.mean(values * values, axis=-1, keepdims=True) + eps)


def turn(values, cosine, sine):
    half = values.shape[-1] // 2
    low, high = values[:, :half], values[:, half:]
    return jnp.concatenate([low * cosine - high * sine, high * cosine + low * sine], axis=-1)


def dot(a, b):
    return jnp.dot(a, b, preferred_element_type=F32)


def dot_t(a, b):
    return lax.dot_general(a, b, (((1,), (1,)), ((), ())), preferred_element_type=F32)


def prep_kernel(
    table, prefix_len, head_at, hidden, in_gain, w_kv, k_gain, frequency, pool,
    normed, fresh, seq, cosine, sine, fresh_all, old, sem, *, n_pages, page, rows, kv_heads,
):
    step = pl.program_id(0)
    steps = pl.num_programs(0)
    head = head_at[0]
    length = prefix_len[0]
    tile = hidden.shape[0]
    total = seq.shape[0]
    prefix = n_pages * page

    def page_copy(p):
        return pltpu.make_async_copy(
            pool.at[table[p], head], old.at[pl.ds(p * page, page)], sem.at[p]
        )

    @pl.when(step == 0)
    def _():
        for p in range(n_pages):
            page_copy(p).start()

    values = (rms_scale(hidden[...].astype(F32)) * in_gain[...]).astype(BF16)
    normed[...] = values
    own = rms_scale(dot(values, w_kv[...]))
    position = length + step * tile + lax.broadcasted_iota(jnp.int32, (tile, 1), 0)
    angles = position.astype(F32) * frequency[...]
    cos, sin = jnp.cos(angles), jnp.sin(angles)
    cosine[...] = cos
    sine[...] = sin
    key = turn(own * k_gain[...], cos, sin)
    slot = jnp.where(head < kv_heads, key, own).astype(BF16)
    fresh[...] = slot
    fresh_all[pl.ds(pl.multiple_of(step * tile, tile), tile), :] = slot

    @pl.when(step == 0)
    def _():
        for p in range(n_pages):
            page_copy(p).wait()
        for p in range(n_pages):
            at = p * page + lax.broadcasted_iota(jnp.int32, (page, 1), 0)
            part = old[p * page : (p + 1) * page, :].astype(F32)
            seq[p * page : (p + 1) * page, :] = jnp.where(at < length, part, 0.0).astype(BF16)
        seq[prefix:total, :] = jnp.zeros((total - prefix, seq.shape[1]), BF16)

    @pl.when(step == steps - 1)
    def _():
        span = rows + page
        base = jnp.minimum(length // page * page, total - span)
        base = pl.multiple_of(base, page)
        row = base + lax.broadcasted_iota(jnp.int32, (span, 1), 0)
        col = lax.broadcasted_iota(jnp.int32, (span, rows), 1)
        pick = jnp.where(row - length == col, 1.0, 0.0).astype(BF16)
        placed = dot(pick, fresh_all[...])
        window = seq[pl.ds(base, span), :].astype(F32)
        seq[pl.ds(base, span), :] = jnp.where(row < length, window, placed).astype(BF16)


def query_kernel(normed, w_q, q_gain, cosine, sine, queries):
    part = rms_scale(dot(normed[...], w_q[...])) * q_gain[...]
    queries[0] = turn(part, cosine[...], sine[...]).astype(BF16)


def attend_kernel(
    table, prefix_len, head_at, send_q, mine_q, w_out, pool, fresh, via_chip, via_core, via_both,
    send, mine, keys, vals, sem, *, own_chip, n_pages, page, kv_heads, group,
):
    head = head_at[0]
    length = prefix_len[0]
    heads, tile, _ = send_q.shape
    kv_of = head * heads // group
    prefix = n_pages * page
    rows = fresh.shape[0]

    copies = []
    for i, buf, slot in ((0, keys, kv_of), (1, vals, kv_of + kv_heads)):
        for p in range(n_pages):
            copies.append(
                pltpu.make_async_copy(
                    pool.at[table[p], slot], buf.at[pl.ds(p * page, page)], sem.at[i, p]
                )
            )
    for copy in copies:
        copy.start()
    sources = (
        (fresh, via_chip),
        (via_core, via_both),
        (via_both, via_core),
        (via_chip, fresh),
    )
    for h, (key_src, val_src) in enumerate(sources):

        @pl.when(head == h)
        def _():
            new_key = pltpu.make_async_copy(
                key_src, keys.at[pl.ds(prefix, rows)], sem.at[0, n_pages]
            )
            new_val = pltpu.make_async_copy(
                val_src, vals.at[pl.ds(prefix, rows)], sem.at[1, n_pages]
            )
            new_key.start()
            new_val.start()
            new_key.wait()
            new_val.wait()

    for copy in copies:
        copy.wait()

    col = lax.broadcasted_iota(jnp.int32, (1, prefix + rows), 1)
    lowest = jnp.where(col < prefix, jnp.where(col < length, -1, rows), col - prefix)
    row = lax.broadcasted_iota(jnp.int32, (tile, 1), 0)
    attns = [[], []]
    for h in range(heads):
        both = jnp.concatenate([send_q[h], mine_q[h]], axis=0)
        token = jnp.concatenate(
            [quarter_of(own_chip, i, head) * tile + row for i in range(2)], axis=0
        )
        scores = jnp.where(lowest <= token, dot_t(both, keys[...]), -jnp.inf)
        top = jnp.max(scores, axis=1, keepdims=True)
        expo = jnp.exp(scores - top)
        total = jnp.sum(expo, axis=1, keepdims=True)
        attns[h] = (dot(expo.astype(BF16), vals[...]) / total).astype(BF16)
    part = dot(jnp.concatenate(attns, axis=1), w_out[...]).astype(BF16)

    send[...] = part[:tile]
    mine[...] = part[tile:]


def quarter_of(own_chip, own_core, head):
    core = head % 2 if own_core else 1 - head % 2
    chip = head // 2 if own_chip else 1 - head // 2
    return chip * 2 + core


def post_kernel(
    head_at, hidden, normed, mine, partner, far, plane, post_gain, left, right, laurel_gain,
    gate, proj, pl_gain, mixed,
):
    total = mine[...].astype(F32) + partner[...].astype(F32) + far[...].astype(F32)
    low = dot_t(normed[...], left[...]).astype(BF16)
    laurel = normed[...].astype(F32) + rms_scale(dot(low, right[...])) * laurel_gain[...]
    state = (hidden[...].astype(F32) + rms_scale(total) * post_gain[...] + laurel) * 2.0 ** (-0.5)
    gated = jax.nn.gelu(dot(state.astype(BF16), gate[...]), approximate=True)
    gated = (gated * plane[...].astype(F32)).astype(BF16)
    mixed[...] = (state + rms_scale(dot(gated, proj[...])) * pl_gain[...]).astype(BF16)


def permute_kernel(owner, spread, after, arranged):
    def place(r, carry):
        arranged[owner[r]] = spread[r]
        return carry

    lax.fori_loop(0, spread.shape[0], place, 0, unroll=8)


def whole(shape):
    zeros = (0,) * len(shape)
    return pl.BlockSpec(shape, lambda *_: zeros)


def on_device(
    hidden_in, layer_input, in_gain, w_query, w_keyval, q_gain, k_gain, w_out, post_gain,
    laurel_left, laurel_right, laurel_gain, w_plgate, w_plproj, pl_gain, kv_pool, page_table,
    prefix_len, decode_owner,
):
    rows, width = hidden_in.shape
    dim = kv_pool.shape[3]
    page = kv_pool.shape[2]
    n_pages = page_table.shape[1]
    kv_heads = kv_pool.shape[1] // 2
    heads = w_query.shape[1] // dim
    prefix = n_pages * page
    total_len = prefix + rows
    blocks = lax.axis_size("blk")
    group = QH // KVH
    n_head = lax.axis_size("head")
    quarter = rows // n_head
    head = lax.axis_index("head").astype(jnp.int32)
    half = dim // 2
    frequency = (rope_base ** (-jnp.arange(half, dtype=F32) / half))[None]
    scalars = (page_table[0], prefix_len, head[None])

    in_gain, q_gain, k_gain = in_gain[None], q_gain[None], k_gain[None]
    post_gain, laurel_gain, pl_gain = post_gain[None], laurel_gain[None], pl_gain[None]

    tile = rows // 2
    normed, fresh, full_seq, cosine, sine = pl.pallas_call(
        functools.partial(
            prep_kernel, n_pages=n_pages, page=page, rows=rows, kv_heads=kv_heads
        ),
        grid_spec=pltpu.PrefetchScalarGridSpec(
            num_scalar_prefetch=3,
            grid=(rows // tile,),
            in_specs=[
                pl.BlockSpec((tile, width), lambda i, *_: (i, 0)),
                whole((1, width)),
                whole((width, dim)),
                whole((1, dim)),
                whole((1, half)),
                pl.BlockSpec(memory_space=ANY),
            ],
            out_specs=[
                pl.BlockSpec((tile, width), lambda i, *_: (i, 0)),
                pl.BlockSpec((tile, dim), lambda i, *_: (i, 0)),
                whole((total_len, dim)),
                pl.BlockSpec((tile, half), lambda i, *_: (i, 0)),
                pl.BlockSpec((tile, half), lambda i, *_: (i, 0)),
            ],
            scratch_shapes=[
                pltpu.VMEM((rows, dim), BF16),
                pltpu.VMEM((prefix, dim), BF16),
                pltpu.SemaphoreType.DMA((n_pages,)),
            ],
        ),
        out_shape=[
            jax.ShapeDtypeStruct((rows, width), BF16),
            jax.ShapeDtypeStruct((rows, dim), BF16),
            jax.ShapeDtypeStruct((total_len, dim), BF16),
            jax.ShapeDtypeStruct((rows, half), F32),
            jax.ShapeDtypeStruct((rows, half), F32),
        ],
        name="prep",
    )(*scalars, hidden_in, in_gain, w_keyval, k_gain, frequency, kv_pool)

    def pairs(moves):
        return [(b * n_head + s, b * n_head + t) for b in range(blocks) for s, t in moves]

    via_chip = lax.ppermute(fresh, AXES, pairs(((1, 3), (2, 0))))
    via_core = lax.ppermute(fresh, AXES, pairs(((0, 1), (3, 2))))
    via_both = lax.ppermute(via_chip, AXES, pairs(((0, 1), (3, 2))))
    spread = lax.all_to_all(
        full_seq.reshape(blocks, total_len // blocks, dim), "blk", 0, 0, tiled=True
    )

    queries = pl.pallas_call(
        query_kernel,
        grid=(heads,),
        in_specs=[
            whole((rows, width)),
            pl.BlockSpec((width, dim), lambda i: (0, i)),
            whole((1, dim)),
            whole((rows, half)),
            whole((rows, half)),
        ],
        out_specs=pl.BlockSpec((1, rows, dim), lambda i: (i, 0, 0)),
        out_shape=jax.ShapeDtypeStruct((heads, rows, dim), BF16),
        name="query",
    )(normed, w_query, q_gain, cosine, sine)

    def attend(own_chip):
        def query_spec(own_core):
            return pl.BlockSpec(
                (heads, quarter, dim),
                lambda i, t, n, h: (0, quarter_of(own_chip, own_core, h[0]), 0),
            )

        return pl.pallas_call(
            functools.partial(
                attend_kernel, own_chip=own_chip, n_pages=n_pages, page=page,
                kv_heads=kv_heads, group=group,
            ),
            grid_spec=pltpu.PrefetchScalarGridSpec(
                num_scalar_prefetch=3,
                grid=(1,),
                in_specs=[query_spec(False), query_spec(True), whole(w_out.shape)]
                + [pl.BlockSpec(memory_space=ANY)] * 5,
                out_specs=[whole((quarter, width))] * 2,
                scratch_shapes=[
                    pltpu.VMEM((total_len, dim), BF16),
                    pltpu.VMEM((total_len, dim), BF16),
                    pltpu.SemaphoreType.DMA((2, n_pages + 1)),
                ],
            ),
            out_shape=[jax.ShapeDtypeStruct((quarter, width), BF16)] * 2,
            name="attend_own" if own_chip else "attend_other",
        )(*scalars, queries, queries, w_out, kv_pool, fresh, via_chip, via_core, via_both)

    core_pairs = pairs(((0, 1), (1, 0), (2, 3), (3, 2)))
    chip_pairs = pairs(((0, 2), (1, 3), (2, 0), (3, 1)))
    send, mine = attend(False)
    partner = lax.ppermute(send, AXES, core_pairs)
    pair_sum = (mine.astype(F32) + partner.astype(F32)).astype(BF16)
    far = lax.ppermute(pair_sum, AXES, chip_pairs)
    send, mine = attend(True)
    partner = lax.ppermute(send, AXES, core_pairs)

    mixed = pl.pallas_call(
        post_kernel,
        grid_spec=pltpu.PrefetchScalarGridSpec(
            num_scalar_prefetch=1,
            grid=(1,),
            in_specs=[
                pl.BlockSpec((quarter, width), lambda i, h: (h[0], 0)),
                pl.BlockSpec((quarter, width), lambda i, h: (h[0], 0)),
                whole((quarter, width)),
                whole((quarter, width)),
                whole((quarter, width)),
                whole(layer_input.shape),
                whole((1, width)),
                whole(laurel_left.shape[::-1]),
                whole(laurel_right.shape),
                whole((1, width)),
                whole(w_plgate.shape),
                whole(w_plproj.shape),
                whole((1, width)),
            ],
            out_specs=whole((quarter, width)),
        ),
        out_shape=jax.ShapeDtypeStruct((quarter, width), BF16),
        name="post",
    )(
        scalars[2], hidden_in, normed, mine, partner, far, layer_input, post_gain, laurel_left.T,
        laurel_right, laurel_gain, w_plgate, w_plproj, pl_gain,
    )

    arranged = pl.pallas_call(
        permute_kernel,
        grid_spec=pltpu.PrefetchScalarGridSpec(
            num_scalar_prefetch=1,
            grid=(1,),
            in_specs=[whole(spread.shape), pl.BlockSpec(memory_space=ANY)],
            out_specs=whole(spread.shape),
        ),
        out_shape=jax.ShapeDtypeStruct(spread.shape, spread.dtype),
        name="permute",
    )(decode_owner, spread, mine)
    owned = lax.all_to_all(arranged, "blk", 0, 0, tiled=True)
    return mixed, owned.reshape(1, 1, total_len, dim)


def solution(mesh):
    in_specs = (
        P("blk", None),
        P(("blk", "head"), None),
        P(),
        P(None, "head"),
        P(None, "head"),
        P(),
        P(),
        P("head", None),
        P(),
        P(),
        P(),
        P(),
        P(),
        P(),
        P(),
        P("blk", None, None, None),
        P("blk", None),
        P("blk"),
        P(),
    )
    out_specs = (P(("blk", "head"), None), P("head", "blk", None, None))
    return jax.shard_map(
        on_device, mesh=mesh, in_specs=in_specs, out_specs=out_specs, check_vma=False
    )
```

```python
import functools

import jax
import jax.numpy as jnp
from jax import lax
from jax.experimental import pallas as pl
from jax.experimental.pallas import tpu as pltpu
from jax.sharding import PartitionSpec as P

QH = 8
KVH = 2
eps = 1e-06
rope_base = 1000000.0
F32 = jnp.float32
BF16 = jnp.bfloat16
ANY = pl.ANY
AXES = ("blk", "head")


def rms_scale(values):
    return values * lax.rsqrt(jnp.mean(values * values, axis=-1, keepdims=True) + eps)


def turn(values, cosine, sine):
    half = values.shape[-1] // 2
    low, high = values[:, :half], values[:, half:]
    return jnp.concatenate([low * cosine - high * sine, high * cosine + low * sine], axis=-1)


def dot(a, b):
    return jnp.dot(a, b, preferred_element_type=F32)


def dot_t(a, b):
    return lax.dot_general(a, b, (((1,), (1,)), ((), ())), preferred_element_type=F32)


def prep_kernel(
    table, prefix_len, head_at, hidden, in_gain, w_kv, k_gain, frequency, pool,
    normed, fresh, seq, cosine, sine, fresh_all, sem, *, n_pages, page, rows, kv_heads,
):
    step = pl.program_id(0)
    steps = pl.num_programs(0)
    head = head_at[0]
    length = prefix_len[0]
    tile = hidden.shape[0]
    total = seq.shape[0]
    prefix = n_pages * page

    def page_copy(p):
        return pltpu.make_async_copy(
            pool.at[table[p], head], seq.at[pl.ds(p * page, page)], sem.at[p]
        )

    @pl.when(step == 0)
    def _():
        for p in range(n_pages):
            page_copy(p).start()

    values = (rms_scale(hidden[...].astype(F32)) * in_gain[...]).astype(BF16)
    normed[...] = values
    own = rms_scale(dot(values, w_kv[...]))
    fine = 16
    at = lax.broadcasted_iota(jnp.int32, (tile // fine, 1), 0)
    coarse_angle = (length + step * tile + at * fine).astype(F32) * frequency[...]
    at = lax.broadcasted_iota(jnp.int32, (fine, 1), 0)
    fine_angle = at.astype(F32) * frequency[...]
    cos_a, sin_a = jnp.cos(coarse_angle)[:, None], jnp.sin(coarse_angle)[:, None]
    cos_b, sin_b = jnp.cos(fine_angle)[None], jnp.sin(fine_angle)[None]
    cos = (cos_a * cos_b - sin_a * sin_b).reshape(tile, -1)
    sin = (sin_a * cos_b + cos_a * sin_b).reshape(tile, -1)
    cosine[...] = cos
    sine[...] = sin
    key = turn(own * k_gain[...], cos, sin)
    slot = jnp.where(head < kv_heads, key, own).astype(BF16)
    fresh[...] = slot
    fresh_all[pl.ds(pl.multiple_of(step * tile, tile), tile), :] = slot

    @pl.when(step == 0)
    def _():
        for p in range(n_pages):
            page_copy(p).wait()
        for p in range(n_pages):

            @pl.when(length <= p * page)
            def _():
                seq[p * page : (p + 1) * page, :] = jnp.zeros((page, seq.shape[1]), BF16)

        seq[prefix:total, :] = jnp.zeros((total - prefix, seq.shape[1]), BF16)

    @pl.when(step == steps - 1)
    def _():
        span = rows + page
        base = jnp.minimum(length // page * page, total - span)
        base = pl.multiple_of(base, page)
        row = base + lax.broadcasted_iota(jnp.int32, (span, 1), 0)
        col = lax.broadcasted_iota(jnp.int32, (span, rows), 1)
        pick = jnp.where(row - length == col, 1.0, 0.0).astype(BF16)
        placed = dot(pick, fresh_all[...])
        window = seq[pl.ds(base, span), :].astype(F32)
        seq[pl.ds(base, span), :] = jnp.where(row < length, window, placed).astype(BF16)


def query_kernel(normed, w_q, q_gain, cosine, sine, queries):
    part = rms_scale(dot(normed[...], w_q[...])) * q_gain[...]
    queries[0] = turn(part, cosine[...], sine[...]).astype(BF16)


def attend_kernel(
    table, prefix_len, head_at, send_q, mine_q, w_out, pool, fresh, via_chip, via_core, via_both,
    send, mine, keys, vals, sem, *, own_chip, n_pages, page, kv_heads, group,
):
    head = head_at[0]
    length = prefix_len[0]
    heads, tile, _ = send_q.shape
    kv_of = head * heads // group
    prefix = n_pages * page
    rows = fresh.shape[0]

    copies = []
    for i, buf, slot in ((0, keys, kv_of), (1, vals, kv_of + kv_heads)):
        for p in range(n_pages):
            copies.append(
                pltpu.make_async_copy(
                    pool.at[table[p], slot], buf.at[pl.ds(p * page, page)], sem.at[i, p]
                )
            )
    for copy in copies:
        copy.start()
    sources = (
        (fresh, via_chip),
        (via_core, via_both),
        (via_both, via_core),
        (via_chip, fresh),
    )
    for h, (key_src, val_src) in enumerate(sources):

        @pl.when(head == h)
        def _():
            new_key = pltpu.make_async_copy(
                key_src, keys.at[pl.ds(prefix, rows)], sem.at[0, n_pages]
            )
            new_val = pltpu.make_async_copy(
                val_src, vals.at[pl.ds(prefix, rows)], sem.at[1, n_pages]
            )
            new_key.start()
            new_val.start()
            new_key.wait()
            new_val.wait()

    for copy in copies:
        copy.wait()

    col = lax.broadcasted_iota(jnp.int32, (1, prefix + rows), 1)
    lowest = jnp.where(col < prefix, jnp.where(col < length, -1, rows), col - prefix)
    row = lax.broadcasted_iota(jnp.int32, (tile, 1), 0)
    attns = [[], []]
    for h in range(heads):
        both = jnp.concatenate([send_q[h], mine_q[h]], axis=0)
        token = jnp.concatenate(
            [quarter_of(own_chip, i, head) * tile + row for i in range(2)], axis=0
        )
        scores = jnp.where(lowest <= token, dot_t(both, keys[...]), -jnp.inf)
        top = jnp.max(scores, axis=1, keepdims=True)
        expo = jnp.exp(scores - top)
        total = jnp.sum(expo, axis=1, keepdims=True)
        attns[h] = (dot(expo.astype(BF16), vals[...]) / total).astype(BF16)
    part = dot(jnp.concatenate(attns, axis=1), w_out[...]).astype(BF16)

    send[...] = part[:tile]
    mine[...] = part[tile:]


def quarter_of(own_chip, own_core, head):
    core = head % 2 if own_core else 1 - head % 2
    chip = head // 2 if own_chip else 1 - head // 2
    return chip * 2 + core


def post_kernel(
    head_at, hidden, normed, mine, partner, far, plane, post_gain, left, right, laurel_gain,
    gate, proj, pl_gain, mixed,
):
    total = mine[...].astype(F32) + partner[...].astype(F32) + far[...].astype(F32)
    low = dot_t(normed[...], left[...]).astype(BF16)
    laurel = normed[...].astype(F32) + rms_scale(dot(low, right[...])) * laurel_gain[...]
    state = (hidden[...].astype(F32) + rms_scale(total) * post_gain[...] + laurel) * 2.0 ** (-0.5)
    gated = jax.nn.gelu(dot(state.astype(BF16), gate[...]), approximate=True)
    gated = (gated * plane[...].astype(F32)).astype(BF16)
    mixed[...] = (state + rms_scale(dot(gated, proj[...])) * pl_gain[...]).astype(BF16)


def permute_kernel(owner, spread, after, arranged):
    def place(r, carry):
        arranged[owner[r]] = spread[r]
        return carry

    lax.fori_loop(0, spread.shape[0], place, 0, unroll=8)


def whole(shape):
    zeros = (0,) * len(shape)
    return pl.BlockSpec(shape, lambda *_: zeros)


def on_device(
    hidden_in, layer_input, in_gain, w_query, w_keyval, q_gain, k_gain, w_out, post_gain,
    laurel_left, laurel_right, laurel_gain, w_plgate, w_plproj, pl_gain, kv_pool, page_table,
    prefix_len, decode_owner,
):
    rows, width = hidden_in.shape
    dim = kv_pool.shape[3]
    page = kv_pool.shape[2]
    n_pages = page_table.shape[1]
    kv_heads = kv_pool.shape[1] // 2
    heads = w_query.shape[1] // dim
    prefix = n_pages * page
    total_len = prefix + rows
    blocks = lax.axis_size("blk")
    group = QH // KVH
    n_head = lax.axis_size("head")
    quarter = rows // n_head
    head = lax.axis_index("head").astype(jnp.int32)
    half = dim // 2
    frequency = (rope_base ** (-jnp.arange(half, dtype=F32) / half))[None]
    scalars = (page_table[0], prefix_len, head[None])

    in_gain, q_gain, k_gain = in_gain[None], q_gain[None], k_gain[None]
    post_gain, laurel_gain, pl_gain = post_gain[None], laurel_gain[None], pl_gain[None]

    tile = rows // 2
    normed, fresh, full_seq, cosine, sine = pl.pallas_call(
        functools.partial(
            prep_kernel, n_pages=n_pages, page=page, rows=rows, kv_heads=kv_heads
        ),
        grid_spec=pltpu.PrefetchScalarGridSpec(
            num_scalar_prefetch=3,
            grid=(rows // tile,),
            in_specs=[
                pl.BlockSpec((tile, width), lambda i, *_: (i, 0)),
                whole((1, width)),
                whole((width, dim)),
                whole((1, dim)),
                whole((1, half)),
                pl.BlockSpec(memory_space=ANY),
            ],
            out_specs=[
                pl.BlockSpec((tile, width), lambda i, *_: (i, 0)),
                pl.BlockSpec((tile, dim), lambda i, *_: (i, 0)),
                whole((total_len, dim)),
                pl.BlockSpec((tile, half), lambda i, *_: (i, 0)),
                pl.BlockSpec((tile, half), lambda i, *_: (i, 0)),
            ],
            scratch_shapes=[
                pltpu.VMEM((rows, dim), BF16),
                pltpu.SemaphoreType.DMA((n_pages,)),
            ],
        ),
        out_shape=[
            jax.ShapeDtypeStruct((rows, width), BF16),
            jax.ShapeDtypeStruct((rows, dim), BF16),
            jax.ShapeDtypeStruct((total_len, dim), BF16),
            jax.ShapeDtypeStruct((rows, half), F32),
            jax.ShapeDtypeStruct((rows, half), F32),
        ],
        name="prep",
    )(*scalars, hidden_in, in_gain, w_keyval, k_gain, frequency, kv_pool)

    def pairs(moves):
        return [(b * n_head + s, b * n_head + t) for b in range(blocks) for s, t in moves]

    via_chip = lax.ppermute(fresh, AXES, pairs(((1, 3), (2, 0))))
    via_core = lax.ppermute(fresh, AXES, pairs(((0, 1), (3, 2))))
    via_both = lax.ppermute(via_chip, AXES, pairs(((0, 1), (3, 2))))
    spread = lax.all_to_all(
        full_seq.reshape(blocks, total_len // blocks, dim), "blk", 0, 0, tiled=True
    )

    queries = pl.pallas_call(
        query_kernel,
        grid=(heads,),
        in_specs=[
            whole((rows, width)),
            pl.BlockSpec((width, dim), lambda i: (0, i)),
            whole((1, dim)),
            whole((rows, half)),
            whole((rows, half)),
        ],
        out_specs=pl.BlockSpec((1, rows, dim), lambda i: (i, 0, 0)),
        out_shape=jax.ShapeDtypeStruct((heads, rows, dim), BF16),
        name="query",
    )(normed, w_query, q_gain, cosine, sine)

    def attend(own_chip):
        def query_spec(own_core):
            return pl.BlockSpec(
                (heads, quarter, dim),
                lambda i, t, n, h: (0, quarter_of(own_chip, own_core, h[0]), 0),
            )

        return pl.pallas_call(
            functools.partial(
                attend_kernel, own_chip=own_chip, n_pages=n_pages, page=page,
                kv_heads=kv_heads, group=group,
            ),
            grid_spec=pltpu.PrefetchScalarGridSpec(
                num_scalar_prefetch=3,
                grid=(1,),
                in_specs=[query_spec(False), query_spec(True), whole(w_out.shape)]
                + [pl.BlockSpec(memory_space=ANY)] * 5,
                out_specs=[whole((quarter, width))] * 2,
                scratch_shapes=[
                    pltpu.VMEM((total_len, dim), BF16),
                    pltpu.VMEM((total_len, dim), BF16),
                    pltpu.SemaphoreType.DMA((2, n_pages + 1)),
                ],
            ),
            out_shape=[jax.ShapeDtypeStruct((quarter, width), BF16)] * 2,
            name="attend_own" if own_chip else "attend_other",
        )(*scalars, queries, queries, w_out, kv_pool, fresh, via_chip, via_core, via_both)

    core_pairs = pairs(((0, 1), (1, 0), (2, 3), (3, 2)))
    chip_pairs = pairs(((0, 2), (1, 3), (2, 0), (3, 1)))
    send, mine = attend(False)
    partner = lax.ppermute(send, AXES, core_pairs)
    pair_sum = (mine.astype(F32) + partner.astype(F32)).astype(BF16)
    far = lax.ppermute(pair_sum, AXES, chip_pairs)
    send, mine = attend(True)
    partner = lax.ppermute(send, AXES, core_pairs)

    mixed = pl.pallas_call(
        post_kernel,
        grid_spec=pltpu.PrefetchScalarGridSpec(
            num_scalar_prefetch=1,
            grid=(1,),
            in_specs=[
                pl.BlockSpec((quarter, width), lambda i, h: (h[0], 0)),
                pl.BlockSpec((quarter, width), lambda i, h: (h[0], 0)),
                whole((quarter, width)),
                whole((quarter, width)),
                whole((quarter, width)),
                whole(layer_input.shape),
                whole((1, width)),
                whole(laurel_left.shape[::-1]),
                whole(laurel_right.shape),
                whole((1, width)),
                whole(w_plgate.shape),
                whole(w_plproj.shape),
                whole((1, width)),
            ],
            out_specs=whole((quarter, width)),
        ),
        out_shape=jax.ShapeDtypeStruct((quarter, width), BF16),
        name="post",
    )(
        scalars[2], hidden_in, normed, mine, partner, far, layer_input, post_gain, laurel_left.T,
        laurel_right, laurel_gain, w_plgate, w_plproj, pl_gain,
    )

    arranged = pl.pallas_call(
        permute_kernel,
        grid_spec=pltpu.PrefetchScalarGridSpec(
            num_scalar_prefetch=1,
            grid=(1,),
            in_specs=[whole(spread.shape), pl.BlockSpec(memory_space=ANY)],
            out_specs=whole(spread.shape),
        ),
        out_shape=jax.ShapeDtypeStruct(spread.shape, spread.dtype),
        name="permute",
    )(decode_owner, spread, pair_sum)
    owned = lax.all_to_all(arranged, "blk", 0, 0, tiled=True)
    return mixed, owned.reshape(1, 1, total_len, dim)


def solution(mesh):
    in_specs = (
        P("blk", None),
        P(("blk", "head"), None),
        P(),
        P(None, "head"),
        P(None, "head"),
        P(),
        P(),
        P("head", None),
        P(),
        P(),
        P(),
        P(),
        P(),
        P(),
        P(),
        P("blk", None, None, None),
        P("blk", None),
        P("blk"),
        P(),
    )
    out_specs = (P(("blk", "head"), None), P("head", "blk", None, None))
    return jax.shard_map(
        on_device, mesh=mesh, in_specs=in_specs, out_specs=out_specs, check_vma=False
    )
```

```python
import functools

import jax
import jax.numpy as jnp
from jax import lax
from jax.experimental import pallas as pl
from jax.experimental.pallas import tpu as pltpu
from jax.sharding import PartitionSpec as P

QH = 8
KVH = 2
eps = 1e-06
rope_base = 1000000.0
F32 = jnp.float32
BF16 = jnp.bfloat16
ANY = pl.ANY
AXES = ("blk", "head")


def rms_scale(values):
    return values * lax.rsqrt(jnp.mean(values * values, axis=-1, keepdims=True) + eps)


def turn(values, cosine, sine):
    half = values.shape[-1] // 2
    low, high = values[:, :half], values[:, half:]
    return jnp.concatenate([low * cosine - high * sine, high * cosine + low * sine], axis=-1)


def dot(a, b):
    return jnp.dot(a, b, preferred_element_type=F32)


def dot_t(a, b):
    return lax.dot_general(a, b, (((1,), (1,)), ((), ())), preferred_element_type=F32)


def prep_kernel(
    table, prefix_len, head_at, hidden, in_gain, w_kv, k_gain, frequency, pool,
    normed, fresh, seq, cosine, sine, fresh_all, sem, *, n_pages, page, rows, kv_heads,
):
    step = pl.program_id(0)
    steps = pl.num_programs(0)
    head = head_at[0]
    length = prefix_len[0]
    tile = hidden.shape[0]
    total = seq.shape[0]
    prefix = n_pages * page

    def page_copy(p):
        return pltpu.make_async_copy(
            pool.at[table[p], head], seq.at[pl.ds(p * page, page)], sem.at[p]
        )

    @pl.when(step == 0)
    def _():
        for p in range(n_pages):
            page_copy(p).start()

    values = (rms_scale(hidden[...].astype(F32)) * in_gain[...]).astype(BF16)
    normed[...] = values
    own = rms_scale(dot(values, w_kv[...]))
    fine = 16
    at = lax.broadcasted_iota(jnp.int32, (tile // fine, 1), 0)
    coarse_angle = (length + step * tile + at * fine).astype(F32) * frequency[...]
    at = lax.broadcasted_iota(jnp.int32, (fine, 1), 0)
    fine_angle = at.astype(F32) * frequency[...]
    cos_a, sin_a = jnp.cos(coarse_angle)[:, None], jnp.sin(coarse_angle)[:, None]
    cos_b, sin_b = jnp.cos(fine_angle)[None], jnp.sin(fine_angle)[None]
    cos = (cos_a * cos_b - sin_a * sin_b).reshape(tile, -1)
    sin = (sin_a * cos_b + cos_a * sin_b).reshape(tile, -1)
    cosine[...] = cos
    sine[...] = sin
    key = turn(own * k_gain[...], cos, sin)
    slot = jnp.where(head < kv_heads, key, own).astype(BF16)
    fresh[...] = slot
    fresh_all[pl.ds(pl.multiple_of(step * tile, tile), tile), :] = slot

    @pl.when(step == 0)
    def _():
        for p in range(n_pages):
            page_copy(p).wait()
        for p in range(n_pages):

            @pl.when(length <= p * page)
            def _():
                seq[p * page : (p + 1) * page, :] = jnp.zeros((page, seq.shape[1]), BF16)

        seq[prefix:total, :] = jnp.zeros((total - prefix, seq.shape[1]), BF16)

    @pl.when(step == steps - 1)
    def _():
        span = rows + page
        base = jnp.minimum(length // page * page, total - span)
        base = pl.multiple_of(base, page)
        row = base + lax.broadcasted_iota(jnp.int32, (span, 1), 0)
        col = lax.broadcasted_iota(jnp.int32, (span, rows), 1)
        pick = jnp.where(row - length == col, 1.0, 0.0).astype(BF16)
        placed = dot(pick, fresh_all[...])
        window = seq[pl.ds(base, span), :].astype(F32)
        seq[pl.ds(base, span), :] = jnp.where(row < length, window, placed).astype(BF16)


def query_kernel(normed, w_q, q_gain, cosine, sine, queries):
    part = rms_scale(dot(normed[...], w_q[...])) * q_gain[...]
    queries[0] = turn(part, cosine[...], sine[...]).astype(BF16)


def old_copies(table, pool, keys, vals, sem, kv_of, kv_heads, n_pages, page):
    return [
        pltpu.make_async_copy(
            pool.at[table[p], slot], buf.at[pl.ds(p * page, page)], sem.at[i, p]
        )
        for i, buf, slot in ((0, keys, kv_of), (1, vals, kv_of + kv_heads))
        for p in range(n_pages)
    ]


def new_copies(head, fresh, via_ring, via_both, keys, vals, key_sem, val_sem):
    sources = (
        (fresh, via_ring),
        (via_ring, via_both),
        (via_both, via_ring),
        (via_ring, fresh),
    )
    for h, (key_src, val_src) in enumerate(sources):

        @pl.when(head == h)
        def _():
            new_key = pltpu.make_async_copy(key_src, keys, key_sem)
            new_val = pltpu.make_async_copy(val_src, vals, val_sem)
            new_key.start()
            new_val.start()
            new_key.wait()
            new_val.wait()


def attend_old_kernel(
    table, prefix_len, head_at, send_q, mine_q, pool, acc, stat, keys, vals, sem,
    *, n_pages, page, kv_heads, group,
):
    head = head_at[0]
    length = prefix_len[0]
    heads, tile, _ = send_q.shape
    prefix = n_pages * page
    kv_of = head * heads // group
    copies = old_copies(table, pool, keys, vals, sem, kv_of, kv_heads, n_pages, page)
    for copy in copies:
        copy.start()
    for copy in copies:
        copy.wait()
    live = lax.broadcasted_iota(jnp.int32, (1, prefix), 1) < length
    for h in range(heads):
        both = jnp.concatenate([send_q[h], mine_q[h]], axis=0)
        scores = jnp.where(live, dot_t(both, keys[...]), -jnp.inf)
        top = jnp.max(scores, axis=1, keepdims=True)
        expo = jnp.exp(scores - top)
        total = jnp.sum(expo, axis=1, keepdims=True)
        acc[h] = dot(expo.astype(BF16), vals[...])
        half = stat.shape[2] // 2
        stat[h, :, :half] = jnp.broadcast_to(top, (2 * tile, half))
        stat[h, :, half:] = jnp.broadcast_to(total, (2 * tile, half))


def attend_new_kernel(
    head_at, send_q, mine_q, acc, stat, w_out, fresh, via_ring, via_both,
    send, mine, keys, vals, sem,
):
    head = head_at[0]
    heads, tile, _ = send_q.shape
    rows = fresh.shape[0]
    new_copies(head, fresh, via_ring, via_both, keys, vals, sem.at[0], sem.at[1])
    col = lax.broadcasted_iota(jnp.int32, (1, rows), 1)
    row = lax.broadcasted_iota(jnp.int32, (tile, 1), 0)
    token = jnp.concatenate([quarter_of(False, i, head) * tile + row for i in range(2)], axis=0)
    half = stat.shape[2] // 2
    attns = []
    for h in range(heads):
        both = jnp.concatenate([send_q[h], mine_q[h]], axis=0)
        scores = jnp.where(col <= token, dot_t(both, keys[...]), -jnp.inf)
        old_top = stat[h, :, :1]
        top = jnp.maximum(old_top, jnp.max(scores, axis=1, keepdims=True))
        expo = jnp.exp(scores - top)
        fade = jnp.exp(old_top - top)
        total = stat[h, :, half : half + 1] * fade + jnp.sum(expo, axis=1, keepdims=True)
        value = acc[h] * fade + dot(expo.astype(BF16), vals[...])
        attns.append((value / total).astype(BF16))
    part = dot(jnp.concatenate(attns, axis=1), w_out[...]).astype(BF16)
    send[...] = part[:tile]
    mine[...] = part[tile:]


def attend_kernel(
    table, prefix_len, head_at, send_q, mine_q, w_out, pool, fresh, via_ring, via_both,
    send, mine, keys, vals, sem, *, n_pages, page, kv_heads, group,
):
    head = head_at[0]
    length = prefix_len[0]
    heads, tile, _ = send_q.shape
    kv_of = head * heads // group
    prefix = n_pages * page
    rows = fresh.shape[0]

    copies = old_copies(table, pool, keys, vals, sem, kv_of, kv_heads, n_pages, page)
    for copy in copies:
        copy.start()
    new_copies(
        head, fresh, via_ring, via_both, keys.at[pl.ds(prefix, rows)],
        vals.at[pl.ds(prefix, rows)], sem.at[0, n_pages], sem.at[1, n_pages],
    )
    for copy in copies:
        copy.wait()

    col = lax.broadcasted_iota(jnp.int32, (1, prefix + rows), 1)
    lowest = jnp.where(col < prefix, jnp.where(col < length, -1, rows), col - prefix)
    row = lax.broadcasted_iota(jnp.int32, (tile, 1), 0)
    attns = [[], []]
    for h in range(heads):
        both = jnp.concatenate([send_q[h], mine_q[h]], axis=0)
        token = jnp.concatenate(
            [quarter_of(True, i, head) * tile + row for i in range(2)], axis=0
        )
        scores = jnp.where(lowest <= token, dot_t(both, keys[...]), -jnp.inf)
        top = jnp.max(scores, axis=1, keepdims=True)
        expo = jnp.exp(scores - top)
        total = jnp.sum(expo, axis=1, keepdims=True)
        attns[h] = (dot(expo.astype(BF16), vals[...]) / total).astype(BF16)
    part = dot(jnp.concatenate(attns, axis=1), w_out[...]).astype(BF16)

    send[...] = part[:tile]
    mine[...] = part[tile:]


def quarter_of(own_chip, own_core, head):
    core = head % 2 if own_core else 1 - head % 2
    chip = head // 2 if own_chip else 1 - head // 2
    return chip * 2 + core


def post_kernel(
    head_at, hidden, normed, mine, partner, far, plane, post_gain, left, right, laurel_gain,
    gate, proj, pl_gain, mixed,
):
    total = mine[...].astype(F32) + partner[...].astype(F32) + far[...].astype(F32)
    low = dot_t(normed[...], left[...]).astype(BF16)
    laurel = normed[...].astype(F32) + rms_scale(dot(low, right[...])) * laurel_gain[...]
    state = (hidden[...].astype(F32) + rms_scale(total) * post_gain[...] + laurel) * 2.0 ** (-0.5)
    gated = jax.nn.gelu(dot(state.astype(BF16), gate[...]), approximate=True)
    gated = (gated * plane[...].astype(F32)).astype(BF16)
    mixed[...] = (state + rms_scale(dot(gated, proj[...])) * pl_gain[...]).astype(BF16)


def permute_kernel(owner, spread, after, arranged):
    def place(r, carry):
        arranged[owner[r]] = spread[r]
        return carry

    lax.fori_loop(0, spread.shape[0], place, 0, unroll=8)


def whole(shape):
    zeros = (0,) * len(shape)
    return pl.BlockSpec(shape, lambda *_: zeros)


def on_device(
    hidden_in, layer_input, in_gain, w_query, w_keyval, q_gain, k_gain, w_out, post_gain,
    laurel_left, laurel_right, laurel_gain, w_plgate, w_plproj, pl_gain, kv_pool, page_table,
    prefix_len, decode_owner,
):
    rows, width = hidden_in.shape
    dim = kv_pool.shape[3]
    page = kv_pool.shape[2]
    n_pages = page_table.shape[1]
    kv_heads = kv_pool.shape[1] // 2
    heads = w_query.shape[1] // dim
    prefix = n_pages * page
    total_len = prefix + rows
    blocks = lax.axis_size("blk")
    group = QH // KVH
    n_head = lax.axis_size("head")
    quarter = rows // n_head
    head = lax.axis_index("head").astype(jnp.int32)
    half = dim // 2
    frequency = (rope_base ** (-jnp.arange(half, dtype=F32) / half))[None]
    scalars = (page_table[0], prefix_len, head[None])

    in_gain, q_gain, k_gain = in_gain[None], q_gain[None], k_gain[None]
    post_gain, laurel_gain, pl_gain = post_gain[None], laurel_gain[None], pl_gain[None]

    tile = rows // 2
    normed, fresh, full_seq, cosine, sine = pl.pallas_call(
        functools.partial(
            prep_kernel, n_pages=n_pages, page=page, rows=rows, kv_heads=kv_heads
        ),
        grid_spec=pltpu.PrefetchScalarGridSpec(
            num_scalar_prefetch=3,
            grid=(rows // tile,),
            in_specs=[
                pl.BlockSpec((tile, width), lambda i, *_: (i, 0)),
                whole((1, width)),
                whole((width, dim)),
                whole((1, dim)),
                whole((1, half)),
                pl.BlockSpec(memory_space=ANY),
            ],
            out_specs=[
                pl.BlockSpec((tile, width), lambda i, *_: (i, 0)),
                pl.BlockSpec((tile, dim), lambda i, *_: (i, 0)),
                whole((total_len, dim)),
                pl.BlockSpec((tile, half), lambda i, *_: (i, 0)),
                pl.BlockSpec((tile, half), lambda i, *_: (i, 0)),
            ],
            scratch_shapes=[
                pltpu.VMEM((rows, dim), BF16),
                pltpu.SemaphoreType.DMA((n_pages,)),
            ],
        ),
        out_shape=[
            jax.ShapeDtypeStruct((rows, width), BF16),
            jax.ShapeDtypeStruct((rows, dim), BF16),
            jax.ShapeDtypeStruct((total_len, dim), BF16),
            jax.ShapeDtypeStruct((rows, half), F32),
            jax.ShapeDtypeStruct((rows, half), F32),
        ],
        name="prep",
    )(*scalars, hidden_in, in_gain, w_keyval, k_gain, frequency, kv_pool)

    def pairs(moves):
        return [(b * n_head + s, b * n_head + t) for b in range(blocks) for s, t in moves]

    via_ring = lax.ppermute(fresh, AXES, pairs(((0, 1), (1, 3), (3, 2), (2, 0))))
    via_both = lax.ppermute(via_ring, AXES, pairs(((0, 1), (3, 2))))
    spread = lax.all_to_all(
        full_seq.reshape(blocks, total_len // blocks, dim), "blk", 0, 0, tiled=True
    )

    queries = pl.pallas_call(
        query_kernel,
        grid=(heads,),
        in_specs=[
            whole((rows, width)),
            pl.BlockSpec((width, dim), lambda i: (0, i)),
            whole((1, dim)),
            whole((rows, half)),
            whole((rows, half)),
        ],
        out_specs=pl.BlockSpec((1, rows, dim), lambda i: (i, 0, 0)),
        out_shape=jax.ShapeDtypeStruct((heads, rows, dim), BF16),
        name="query",
    )(normed, w_query, q_gain, cosine, sine)

    hbm = pl.BlockSpec(memory_space=ANY)
    parts = [jax.ShapeDtypeStruct((quarter, width), BF16)] * 2
    sizes = dict(n_pages=n_pages, page=page, kv_heads=kv_heads, group=group)
    state = (heads, 2 * quarter, dim)

    def query_specs(own_chip):
        return [
            pl.BlockSpec(
                (heads, quarter, dim),
                lambda i, *m, core=core: (0, quarter_of(own_chip, core, m[-1][0]), 0),
            )
            for core in (False, True)
        ]

    acc, stat = pl.pallas_call(
        functools.partial(attend_old_kernel, **sizes),
        grid_spec=pltpu.PrefetchScalarGridSpec(
            num_scalar_prefetch=3,
            grid=(1,),
            in_specs=query_specs(False) + [hbm],
            out_specs=[whole(state)] * 2,
            scratch_shapes=[
                pltpu.VMEM((prefix, dim), BF16),
                pltpu.VMEM((prefix, dim), BF16),
                pltpu.SemaphoreType.DMA((2, n_pages)),
            ],
        ),
        out_shape=[jax.ShapeDtypeStruct(state, F32)] * 2,
        name="attend_old",
    )(*scalars, queries, queries, kv_pool)

    send, mine = pl.pallas_call(
        attend_new_kernel,
        grid_spec=pltpu.PrefetchScalarGridSpec(
            num_scalar_prefetch=1,
            grid=(1,),
            in_specs=query_specs(False)
            + [whole(state), whole(state), whole(w_out.shape)]
            + [hbm] * 3,
            out_specs=[whole((quarter, width))] * 2,
            scratch_shapes=[
                pltpu.VMEM((rows, dim), BF16),
                pltpu.VMEM((rows, dim), BF16),
                pltpu.SemaphoreType.DMA((2,)),
            ],
        ),
        out_shape=parts,
        name="attend_new",
    )(scalars[2], queries, queries, acc, stat, w_out, fresh, via_ring, via_both)

    core_pairs = pairs(((0, 1), (1, 0), (2, 3), (3, 2)))
    chip_pairs = pairs(((0, 2), (1, 3), (2, 0), (3, 1)))
    partner = lax.ppermute(send, AXES, core_pairs)
    pair_sum = (mine.astype(F32) + partner.astype(F32)).astype(BF16)
    far = lax.ppermute(pair_sum, AXES, chip_pairs)
    send, mine = pl.pallas_call(
        functools.partial(attend_kernel, **sizes),
        grid_spec=pltpu.PrefetchScalarGridSpec(
            num_scalar_prefetch=3,
            grid=(1,),
            in_specs=query_specs(True) + [whole(w_out.shape)] + [hbm] * 4,
            out_specs=[whole((quarter, width))] * 2,
            scratch_shapes=[
                pltpu.VMEM((total_len, dim), BF16),
                pltpu.VMEM((total_len, dim), BF16),
                pltpu.SemaphoreType.DMA((2, n_pages + 1)),
            ],
        ),
        out_shape=parts,
        name="attend_own",
    )(*scalars, queries, queries, w_out, kv_pool, fresh, via_ring, via_both)
    partner = lax.ppermute(send, AXES, core_pairs)

    mixed = pl.pallas_call(
        post_kernel,
        grid_spec=pltpu.PrefetchScalarGridSpec(
            num_scalar_prefetch=1,
            grid=(1,),
            in_specs=[
                pl.BlockSpec((quarter, width), lambda i, h: (h[0], 0)),
                pl.BlockSpec((quarter, width), lambda i, h: (h[0], 0)),
                whole((quarter, width)),
                whole((quarter, width)),
                whole((quarter, width)),
                whole(layer_input.shape),
                whole((1, width)),
                whole(laurel_left.shape[::-1]),
                whole(laurel_right.shape),
                whole((1, width)),
                whole(w_plgate.shape),
                whole(w_plproj.shape),
                whole((1, width)),
            ],
            out_specs=whole((quarter, width)),
        ),
        out_shape=jax.ShapeDtypeStruct((quarter, width), BF16),
        name="post",
    )(
        scalars[2], hidden_in, normed, mine, partner, far, layer_input, post_gain, laurel_left.T,
        laurel_right, laurel_gain, w_plgate, w_plproj, pl_gain,
    )

    arranged = pl.pallas_call(
        permute_kernel,
        grid_spec=pltpu.PrefetchScalarGridSpec(
            num_scalar_prefetch=1,
            grid=(1,),
            in_specs=[whole(spread.shape), pl.BlockSpec(memory_space=ANY)],
            out_specs=whole(spread.shape),
        ),
        out_shape=jax.ShapeDtypeStruct(spread.shape, spread.dtype),
        name="permute",
    )(decode_owner, spread, pair_sum)
    owned = lax.all_to_all(arranged, "blk", 0, 0, tiled=True)
    return mixed, owned.reshape(1, 1, total_len, dim)


def solution(mesh):
    in_specs = (
        P("blk", None),
        P(("blk", "head"), None),
        P(),
        P(None, "head"),
        P(None, "head"),
        P(),
        P(),
        P("head", None),
        P(),
        P(),
        P(),
        P(),
        P(),
        P(),
        P(),
        P("blk", None, None, None),
        P("blk", None),
        P("blk"),
        P(),
    )
    out_specs = (P(("blk", "head"), None), P("head", "blk", None, None))
    return jax.shard_map(
        on_device, mesh=mesh, in_specs=in_specs, out_specs=out_specs, check_vma=False
    )
```

```python
import functools

import jax
import jax.numpy as jnp
import numpy as np
from jax import lax
from jax.experimental import pallas as pl
from jax.experimental.pallas import tpu as pltpu
from jax.sharding import PartitionSpec as P

QH = 8
KVH = 2
eps = 1e-06
rope_base = 1000000.0
F32 = jnp.float32
BF16 = jnp.bfloat16
ANY = pl.ANY
AXES = ("blk", "head")


def rms_scale(values):
    return values * lax.rsqrt(jnp.mean(values * values, axis=-1, keepdims=True) + eps)


def turn(values, cosine, sine):
    half = values.shape[-1] // 2
    low, high = values[:, :half], values[:, half:]
    return jnp.concatenate([low * cosine - high * sine, high * cosine + low * sine], axis=-1)


def dot(a, b):
    return jnp.dot(a, b, preferred_element_type=F32)


def dot_t(a, b):
    return lax.dot_general(a, b, (((1,), (1,)), ((), ())), preferred_element_type=F32)


def prep_kernel(
    table, prefix_len, head_at, hidden, in_gain, w_kv, k_gain, frequency, pool,
    normed, fresh, seq, cosine, sine, sem, *, n_pages, page, kv_heads,
):
    step = pl.program_id(0)
    head = head_at[0]
    length = prefix_len[0]
    tile = hidden.shape[0]
    total = seq.shape[0]
    prefix = n_pages * page

    def page_copy(p):
        return pltpu.make_async_copy(
            pool.at[table[p], head], seq.at[pl.ds(p * page, page)], sem.at[p]
        )

    @pl.when(step == 0)
    def _():
        for p in range(n_pages):
            page_copy(p).start()

    values = (rms_scale(hidden[...].astype(F32)) * in_gain[...]).astype(BF16)
    normed[...] = values
    own = rms_scale(dot(values, w_kv[...]))
    fine = 16
    at = lax.broadcasted_iota(jnp.int32, (tile // fine, 1), 0)
    coarse_angle = (length + step * tile + at * fine).astype(F32) * frequency[...]
    at = lax.broadcasted_iota(jnp.int32, (fine, 1), 0)
    fine_angle = at.astype(F32) * frequency[...]
    cos_a, sin_a = jnp.cos(coarse_angle)[:, None], jnp.sin(coarse_angle)[:, None]
    cos_b, sin_b = jnp.cos(fine_angle)[None], jnp.sin(fine_angle)[None]
    cos = (cos_a * cos_b - sin_a * sin_b).reshape(tile, -1)
    sin = (sin_a * cos_b + cos_a * sin_b).reshape(tile, -1)
    cosine[...] = cos
    sine[...] = sin
    key = turn(own * k_gain[...], cos, sin)
    slot = jnp.where(head < kv_heads, key, own).astype(BF16)
    fresh[...] = slot

    @pl.when(step == 0)
    def _():
        for p in range(n_pages):
            page_copy(p).wait()
        for p in range(n_pages):

            @pl.when(length <= p * page)
            def _():
                seq[p * page : (p + 1) * page, :] = jnp.zeros((page, seq.shape[1]), BF16)

        seq[prefix:total, :] = jnp.zeros((total - prefix, seq.shape[1]), BF16)

    start = length + step * tile
    span = tile + page
    base = pl.multiple_of(jnp.minimum(start // page * page, total - span), page)
    row = base + lax.broadcasted_iota(jnp.int32, (span, 1), 0)
    col = lax.broadcasted_iota(jnp.int32, (span, tile), 1)
    pick = jnp.where(row - start == col, 1.0, 0.0).astype(BF16)
    placed = dot(pick, slot)
    window = seq[pl.ds(base, span), :].astype(F32)
    seq[pl.ds(base, span), :] = jnp.where(row < start, window, placed).astype(BF16)


def query_kernel(normed, w_q, q_gain, cosine, sine, queries):
    part = rms_scale(dot(normed[...], w_q[...])) * q_gain[...]
    queries[0] = turn(part, cosine[...], sine[...]).astype(BF16)


def old_copies(table, pool, keys, vals, sem, kv_of, kv_heads, n_pages, page):
    return [
        pltpu.make_async_copy(
            pool.at[table[p], slot], buf.at[pl.ds(p * page, page)], sem.at[i, p]
        )
        for i, buf, slot in ((0, keys, kv_of), (1, vals, kv_of + kv_heads))
        for p in range(n_pages)
    ]


def new_copies(head, fresh, via_ring, via_both, keys, vals, key_sem, val_sem):
    sources = (
        (fresh, via_ring),
        (via_ring, via_both),
        (via_both, via_ring),
        (via_ring, fresh),
    )
    for h, (key_src, val_src) in enumerate(sources):

        @pl.when(head == h)
        def _():
            new_key = pltpu.make_async_copy(key_src, keys, key_sem)
            new_val = pltpu.make_async_copy(val_src, vals, val_sem)
            new_key.start()
            new_val.start()
            new_key.wait()
            new_val.wait()


def attend_old_kernel(
    table, prefix_len, head_at, send_q, mine_q, pool, acc, stat, keys, vals, sem,
    *, n_pages, page, kv_heads, group,
):
    head = head_at[0]
    length = prefix_len[0]
    heads, tile, _ = send_q.shape
    prefix = n_pages * page
    kv_of = head * heads // group
    copies = old_copies(table, pool, keys, vals, sem, kv_of, kv_heads, n_pages, page)
    for copy in copies:
        copy.start()
    for copy in copies:
        copy.wait()
    live = lax.broadcasted_iota(jnp.int32, (1, prefix), 1) < length
    for h in range(heads):
        both = jnp.concatenate([send_q[h], mine_q[h]], axis=0)
        scores = jnp.where(live, dot_t(both, keys[...]), -jnp.inf)
        top = jnp.max(scores, axis=1, keepdims=True)
        expo = jnp.exp(scores - top)
        total = jnp.sum(expo, axis=1, keepdims=True)
        acc[h] = dot(expo.astype(BF16), vals[...])
        half = stat.shape[2] // 2
        stat[h, :, :half] = jnp.broadcast_to(top, (2 * tile, half))
        stat[h, :, half:] = jnp.broadcast_to(total, (2 * tile, half))


def attend_new_kernel(
    head_at, send_q, mine_q, acc, stat, w_out, fresh, via_ring, via_both,
    send, mine, keys, vals, sem,
):
    head = head_at[0]
    heads, tile, _ = send_q.shape
    rows = fresh.shape[0]
    new_copies(head, fresh, via_ring, via_both, keys, vals, sem.at[0], sem.at[1])
    col = lax.broadcasted_iota(jnp.int32, (1, rows), 1)
    row = lax.broadcasted_iota(jnp.int32, (tile, 1), 0)
    token = jnp.concatenate([quarter_of(False, i, head) * tile + row for i in range(2)], axis=0)
    half = stat.shape[2] // 2
    attns = []
    for h in range(heads):
        both = jnp.concatenate([send_q[h], mine_q[h]], axis=0)
        scores = jnp.where(col <= token, dot_t(both, keys[...]), -jnp.inf)
        old_top = stat[h, :, :1]
        top = jnp.maximum(old_top, jnp.max(scores, axis=1, keepdims=True))
        expo = jnp.exp(scores - top)
        fade = jnp.exp(old_top - top)
        total = stat[h, :, half : half + 1] * fade + jnp.sum(expo, axis=1, keepdims=True)
        value = acc[h] * fade + dot(expo.astype(BF16), vals[...])
        attns.append((value / total).astype(BF16))
    part = dot(jnp.concatenate(attns, axis=1), w_out[...]).astype(BF16)
    send[...] = part[:tile]
    mine[...] = part[tile:]


def attend_kernel(
    table, prefix_len, head_at, send_q, mine_q, w_out, pool, fresh, via_ring, via_both,
    send, mine, keys, vals, sem, *, n_pages, page, kv_heads, group,
):
    head = head_at[0]
    length = prefix_len[0]
    heads, tile, _ = send_q.shape
    kv_of = head * heads // group
    prefix = n_pages * page
    rows = fresh.shape[0]

    copies = old_copies(table, pool, keys, vals, sem, kv_of, kv_heads, n_pages, page)
    for copy in copies:
        copy.start()
    new_copies(
        head, fresh, via_ring, via_both, keys.at[pl.ds(prefix, rows)],
        vals.at[pl.ds(prefix, rows)], sem.at[0, n_pages], sem.at[1, n_pages],
    )
    for copy in copies:
        copy.wait()

    col = lax.broadcasted_iota(jnp.int32, (1, prefix + rows), 1)
    lowest = jnp.where(col < prefix, jnp.where(col < length, -1, rows), col - prefix)
    row = lax.broadcasted_iota(jnp.int32, (tile, 1), 0)
    attns = [[], []]
    for h in range(heads):
        both = jnp.concatenate([send_q[h], mine_q[h]], axis=0)
        token = jnp.concatenate(
            [quarter_of(True, i, head) * tile + row for i in range(2)], axis=0
        )
        scores = jnp.where(lowest <= token, dot_t(both, keys[...]), -jnp.inf)
        top = jnp.max(scores, axis=1, keepdims=True)
        expo = jnp.exp(scores - top)
        total = jnp.sum(expo, axis=1, keepdims=True)
        attns[h] = (dot(expo.astype(BF16), vals[...]) / total).astype(BF16)
    part = dot(jnp.concatenate(attns, axis=1), w_out[...]).astype(BF16)

    send[...] = part[:tile]
    mine[...] = part[tile:]


def quarter_of(own_chip, own_core, head):
    core = head % 2 if own_core else 1 - head % 2
    chip = head // 2 if own_chip else 1 - head // 2
    return chip * 2 + core


def post_kernel(
    head_at, hidden, normed, mine, partner, far, plane, post_gain, left, right, laurel_gain,
    gate, proj, pl_gain, mixed,
):
    total = mine[...].astype(F32) + partner[...].astype(F32) + far[...].astype(F32)
    low = dot_t(normed[...], left[...]).astype(BF16)
    laurel = normed[...].astype(F32) + rms_scale(dot(low, right[...])) * laurel_gain[...]
    state = (hidden[...].astype(F32) + rms_scale(total) * post_gain[...] + laurel) * 2.0 ** (-0.5)
    gated = jax.nn.gelu(dot(state.astype(BF16), gate[...]), approximate=True)
    gated = (gated * plane[...].astype(F32)).astype(BF16)
    mixed[...] = (state + rms_scale(dot(gated, proj[...])) * pl_gain[...]).astype(BF16)


def permute_kernel(owner, spread, after, arranged):
    def place(r, carry):
        arranged[owner[r]] = spread[r]
        return carry

    lax.fori_loop(0, spread.shape[0], place, 0, unroll=8)


def whole(shape):
    zeros = (0,) * len(shape)
    return pl.BlockSpec(shape, lambda *_: zeros)


def on_device(
    hidden_in, layer_input, in_gain, w_query, w_keyval, q_gain, k_gain, w_out, post_gain,
    laurel_left, laurel_right, laurel_gain, w_plgate, w_plproj, pl_gain, kv_pool, page_table,
    prefix_len, decode_owner,
):
    rows, width = hidden_in.shape
    dim = kv_pool.shape[3]
    page = kv_pool.shape[2]
    n_pages = page_table.shape[1]
    kv_heads = kv_pool.shape[1] // 2
    heads = w_query.shape[1] // dim
    prefix = n_pages * page
    total_len = prefix + rows
    blocks = lax.axis_size("blk")
    group = QH // KVH
    n_head = lax.axis_size("head")
    quarter = rows // n_head
    head = lax.axis_index("head").astype(jnp.int32)
    half = dim // 2
    frequency = jnp.asarray((rope_base ** (-np.arange(half) / half))[None], F32)
    scalars = (page_table[0], prefix_len, head[None])

    in_gain, q_gain, k_gain = in_gain[None], q_gain[None], k_gain[None]
    post_gain, laurel_gain, pl_gain = post_gain[None], laurel_gain[None], pl_gain[None]

    tile = rows // 2
    normed, fresh, full_seq, cosine, sine = pl.pallas_call(
        functools.partial(
            prep_kernel, n_pages=n_pages, page=page, kv_heads=kv_heads
        ),
        grid_spec=pltpu.PrefetchScalarGridSpec(
            num_scalar_prefetch=3,
            grid=(rows // tile,),
            in_specs=[
                pl.BlockSpec((tile, width), lambda i, *_: (i, 0)),
                whole((1, width)),
                whole((width, dim)),
                whole((1, dim)),
                whole((1, half)),
                pl.BlockSpec(memory_space=ANY),
            ],
            out_specs=[
                pl.BlockSpec((tile, width), lambda i, *_: (i, 0)),
                pl.BlockSpec((tile, dim), lambda i, *_: (i, 0)),
                whole((total_len, dim)),
                pl.BlockSpec((tile, half), lambda i, *_: (i, 0)),
                pl.BlockSpec((tile, half), lambda i, *_: (i, 0)),
            ],
            scratch_shapes=[
                pltpu.SemaphoreType.DMA((n_pages,)),
            ],
        ),
        out_shape=[
            jax.ShapeDtypeStruct((rows, width), BF16),
            jax.ShapeDtypeStruct((rows, dim), BF16),
            jax.ShapeDtypeStruct((total_len, dim), BF16),
            jax.ShapeDtypeStruct((rows, half), F32),
            jax.ShapeDtypeStruct((rows, half), F32),
        ],
        name="prep",
    )(*scalars, hidden_in, in_gain, w_keyval, k_gain, frequency, kv_pool)

    def pairs(moves):
        return [(b * n_head + s, b * n_head + t) for b in range(blocks) for s, t in moves]

    via_ring = lax.ppermute(fresh, AXES, pairs(((0, 1), (1, 3), (3, 2), (2, 0))))
    via_both = lax.ppermute(via_ring, AXES, pairs(((0, 1), (3, 2))))
    spread = lax.all_to_all(
        full_seq.reshape(blocks, total_len // blocks, dim), "blk", 0, 0, tiled=True
    )

    queries = pl.pallas_call(
        query_kernel,
        grid=(heads,),
        in_specs=[
            whole((rows, width)),
            pl.BlockSpec((width, dim), lambda i: (0, i)),
            whole((1, dim)),
            whole((rows, half)),
            whole((rows, half)),
        ],
        out_specs=pl.BlockSpec((1, rows, dim), lambda i: (i, 0, 0)),
        out_shape=jax.ShapeDtypeStruct((heads, rows, dim), BF16),
        name="query",
    )(normed, w_query, q_gain, cosine, sine)

    hbm = pl.BlockSpec(memory_space=ANY)
    parts = [jax.ShapeDtypeStruct((quarter, width), BF16)] * 2
    sizes = dict(n_pages=n_pages, page=page, kv_heads=kv_heads, group=group)
    state = (heads, 2 * quarter, dim)

    def query_specs(own_chip):
        return [
            pl.BlockSpec(
                (heads, quarter, dim),
                lambda i, *m, core=core: (0, quarter_of(own_chip, core, m[-1][0]), 0),
            )
            for core in (False, True)
        ]

    acc, stat = pl.pallas_call(
        functools.partial(attend_old_kernel, **sizes),
        grid_spec=pltpu.PrefetchScalarGridSpec(
            num_scalar_prefetch=3,
            grid=(1,),
            in_specs=query_specs(False) + [hbm],
            out_specs=[whole(state)] * 2,
            scratch_shapes=[
                pltpu.VMEM((prefix, dim), BF16),
                pltpu.VMEM((prefix, dim), BF16),
                pltpu.SemaphoreType.DMA((2, n_pages)),
            ],
        ),
        out_shape=[jax.ShapeDtypeStruct(state, F32)] * 2,
        name="attend_old",
    )(*scalars, queries, queries, kv_pool)

    send, mine = pl.pallas_call(
        attend_new_kernel,
        grid_spec=pltpu.PrefetchScalarGridSpec(
            num_scalar_prefetch=1,
            grid=(1,),
            in_specs=query_specs(False)
            + [whole(state), whole(state), whole(w_out.shape)]
            + [hbm] * 3,
            out_specs=[whole((quarter, width))] * 2,
            scratch_shapes=[
                pltpu.VMEM((rows, dim), BF16),
                pltpu.VMEM((rows, dim), BF16),
                pltpu.SemaphoreType.DMA((2,)),
            ],
        ),
        out_shape=parts,
        name="attend_new",
    )(scalars[2], queries, queries, acc, stat, w_out, fresh, via_ring, via_both)

    core_pairs = pairs(((0, 1), (1, 0), (2, 3), (3, 2)))
    chip_pairs = pairs(((0, 2), (1, 3), (2, 0), (3, 1)))
    partner = lax.ppermute(send, AXES, core_pairs)
    pair_sum = (mine.astype(F32) + partner.astype(F32)).astype(BF16)
    far = lax.ppermute(pair_sum, AXES, chip_pairs)
    send, mine = pl.pallas_call(
        functools.partial(attend_kernel, **sizes),
        grid_spec=pltpu.PrefetchScalarGridSpec(
            num_scalar_prefetch=3,
            grid=(1,),
            in_specs=query_specs(True) + [whole(w_out.shape)] + [hbm] * 4,
            out_specs=[whole((quarter, width))] * 2,
            scratch_shapes=[
                pltpu.VMEM((total_len, dim), BF16),
                pltpu.VMEM((total_len, dim), BF16),
                pltpu.SemaphoreType.DMA((2, n_pages + 1)),
            ],
        ),
        out_shape=parts,
        name="attend_own",
    )(*scalars, queries, queries, w_out, kv_pool, fresh, via_ring, via_both)
    partner = lax.ppermute(send, AXES, core_pairs)

    mixed = pl.pallas_call(
        post_kernel,
        grid_spec=pltpu.PrefetchScalarGridSpec(
            num_scalar_prefetch=1,
            grid=(1,),
            in_specs=[
                pl.BlockSpec((quarter, width), lambda i, h: (h[0], 0)),
                pl.BlockSpec((quarter, width), lambda i, h: (h[0], 0)),
                whole((quarter, width)),
                whole((quarter, width)),
                whole((quarter, width)),
                whole(layer_input.shape),
                whole((1, width)),
                whole(laurel_left.shape[::-1]),
                whole(laurel_right.shape),
                whole((1, width)),
                whole(w_plgate.shape),
                whole(w_plproj.shape),
                whole((1, width)),
            ],
            out_specs=whole((quarter, width)),
        ),
        out_shape=jax.ShapeDtypeStruct((quarter, width), BF16),
        name="post",
    )(
        scalars[2], hidden_in, normed, mine, partner, far, layer_input, post_gain, laurel_left.T,
        laurel_right, laurel_gain, w_plgate, w_plproj, pl_gain,
    )

    arranged = pl.pallas_call(
        permute_kernel,
        grid_spec=pltpu.PrefetchScalarGridSpec(
            num_scalar_prefetch=1,
            grid=(1,),
            in_specs=[whole(spread.shape), pl.BlockSpec(memory_space=ANY)],
            out_specs=whole(spread.shape),
        ),
        out_shape=jax.ShapeDtypeStruct(spread.shape, spread.dtype),
        name="permute",
    )(decode_owner, spread, pair_sum)
    owned = lax.all_to_all(arranged, "blk", 0, 0, tiled=True)
    return mixed, owned.reshape(1, 1, total_len, dim)


def solution(mesh):
    in_specs = (
        P("blk", None),
        P(("blk", "head"), None),
        P(),
        P(None, "head"),
        P(None, "head"),
        P(),
        P(),
        P("head", None),
        P(),
        P(),
        P(),
        P(),
        P(),
        P(),
        P(),
        P("blk", None, None, None),
        P("blk", None),
        P("blk"),
        P(),
    )
    out_specs = (P(("blk", "head"), None), P("head", "blk", None, None))
    return jax.shard_map(
        on_device, mesh=mesh, in_specs=in_specs, out_specs=out_specs, check_vma=False
    )
```

```python
import functools

import jax
import jax.numpy as jnp
import numpy as np
from jax import lax
from jax.experimental import pallas as pl
from jax.experimental.pallas import tpu as pltpu
from jax.sharding import PartitionSpec as P

QH = 8
KVH = 2
eps = 1e-06
rope_base = 1000000.0
F32 = jnp.float32
BF16 = jnp.bfloat16
ANY = pl.ANY
AXES = ("blk", "head")


def rms_scale(values):
    return values * lax.rsqrt(jnp.mean(values * values, axis=-1, keepdims=True) + eps)


def turn(values, cosine, sine):
    half = values.shape[-1] // 2
    low, high = values[:, :half], values[:, half:]
    return jnp.concatenate([low * cosine - high * sine, high * cosine + low * sine], axis=-1)


def dot(a, b):
    return jnp.dot(a, b, preferred_element_type=F32)


def dot_t(a, b):
    return lax.dot_general(a, b, (((1,), (1,)), ((), ())), preferred_element_type=F32)


def prep_kernel(
    table, prefix_len, head_at, hidden, in_gain, w_kv, k_gain, frequency, pool,
    normed, fresh, seq, cosine, sine, weights, sem, *, n_pages, page, kv_heads,
):
    step = pl.program_id(0)
    head = head_at[0]
    length = prefix_len[0]
    tile = hidden.shape[0]
    total = seq.shape[0]
    prefix = n_pages * page

    def page_copy(p):
        return pltpu.make_async_copy(
            pool.at[table[p], head], seq.at[pl.ds(p * page, page)], sem.at[p]
        )

    fetch = pltpu.make_async_copy(w_kv, weights, sem.at[n_pages])

    @pl.when(step == 0)
    def _():
        fetch.start()
        for p in range(n_pages):
            page_copy(p).start()

    values = (rms_scale(hidden[...].astype(F32)) * in_gain[...]).astype(BF16)
    normed[...] = values

    @pl.when(step == 0)
    def _():
        fetch.wait()

    own = rms_scale(dot(values, weights[...]))
    fine = 16
    at = lax.broadcasted_iota(jnp.int32, (tile // fine, 1), 0)
    coarse_angle = (length + step * tile + at * fine).astype(F32) * frequency[...]
    at = lax.broadcasted_iota(jnp.int32, (fine, 1), 0)
    fine_angle = at.astype(F32) * frequency[...]
    cos_a, sin_a = jnp.cos(coarse_angle)[:, None], jnp.sin(coarse_angle)[:, None]
    cos_b, sin_b = jnp.cos(fine_angle)[None], jnp.sin(fine_angle)[None]
    cos = (cos_a * cos_b - sin_a * sin_b).reshape(tile, -1)
    sin = (sin_a * cos_b + cos_a * sin_b).reshape(tile, -1)
    cosine[...] = cos
    sine[...] = sin
    key = turn(own * k_gain[...], cos, sin)
    slot = jnp.where(head < kv_heads, key, own).astype(BF16)
    fresh[...] = slot

    @pl.when(step == 0)
    def _():
        for p in range(n_pages):
            page_copy(p).wait()
        for p in range(n_pages):

            @pl.when(length <= p * page)
            def _():
                seq[p * page : (p + 1) * page, :] = jnp.zeros((page, seq.shape[1]), BF16)

        seq[prefix:total, :] = jnp.zeros((total - prefix, seq.shape[1]), BF16)

    start = length + step * tile
    span = tile + page
    base = pl.multiple_of(jnp.minimum(start // page * page, total - span), page)
    row = base + lax.broadcasted_iota(jnp.int32, (span, 1), 0)
    col = lax.broadcasted_iota(jnp.int32, (span, tile), 1)
    pick = jnp.where(row - start == col, 1.0, 0.0).astype(BF16)
    placed = dot(pick, slot)
    window = seq[pl.ds(base, span), :].astype(F32)
    seq[pl.ds(base, span), :] = jnp.where(row < start, window, placed).astype(BF16)


def query_kernel(normed, w_q, q_gain, cosine, sine, queries):
    part = rms_scale(dot(normed[...], w_q[...])) * q_gain[...]
    queries[0] = turn(part, cosine[...], sine[...]).astype(BF16)


def old_copies(table, pool, keys, vals, sem, kv_of, kv_heads, n_pages, page):
    return [
        pltpu.make_async_copy(
            pool.at[table[p], slot], buf.at[pl.ds(p * page, page)], sem.at[i, p]
        )
        for i, buf, slot in ((0, keys, kv_of), (1, vals, kv_of + kv_heads))
        for p in range(n_pages)
    ]


def new_copies(head, fresh, via_ring, via_both, keys, vals, key_sem, val_sem):
    sources = (
        (fresh, via_ring),
        (via_ring, via_both),
        (via_both, via_ring),
        (via_ring, fresh),
    )
    for h, (key_src, val_src) in enumerate(sources):

        @pl.when(head == h)
        def _():
            new_key = pltpu.make_async_copy(key_src, keys, key_sem)
            new_val = pltpu.make_async_copy(val_src, vals, val_sem)
            new_key.start()
            new_val.start()
            new_key.wait()
            new_val.wait()


def attend_old_kernel(
    table, prefix_len, head_at, send_q, mine_q, pool, acc, stat, keys, vals, sem,
    *, n_pages, page, kv_heads, group,
):
    head = head_at[0]
    length = prefix_len[0]
    heads, tile, _ = send_q.shape
    prefix = n_pages * page
    kv_of = head * heads // group
    copies = old_copies(table, pool, keys, vals, sem, kv_of, kv_heads, n_pages, page)
    for copy in copies:
        copy.start()
    for copy in copies[:n_pages]:
        copy.wait()
    live = lax.broadcasted_iota(jnp.int32, (1, prefix), 1) < length
    for h in range(heads):
        both = jnp.concatenate([send_q[h], mine_q[h]], axis=0)
        scores = jnp.where(live, dot_t(both, keys[...]), -jnp.inf)
        top = jnp.max(scores, axis=1, keepdims=True)
        expo = jnp.exp(scores - top)
        total = jnp.sum(expo, axis=1, keepdims=True)
        if h == 0:
            for copy in copies[n_pages:]:
                copy.wait()
        acc[h] = dot(expo.astype(BF16), vals[...])
        half = stat.shape[2] // 2
        stat[h, :, :half] = jnp.broadcast_to(top, (2 * tile, half))
        stat[h, :, half:] = jnp.broadcast_to(total, (2 * tile, half))


def attend_new_kernel(
    head_at, send_q, mine_q, acc, stat, w_out, fresh, via_ring, via_both,
    send, mine, keys, vals, weights, sem,
):
    head = head_at[0]
    fetch = pltpu.make_async_copy(w_out, weights, sem.at[2])
    heads, tile, _ = send_q.shape
    rows = fresh.shape[0]
    new_copies(head, fresh, via_ring, via_both, keys, vals, sem.at[0], sem.at[1])
    fetch.start()
    col = lax.broadcasted_iota(jnp.int32, (1, rows), 1)
    row = lax.broadcasted_iota(jnp.int32, (tile, 1), 0)
    token = jnp.concatenate([quarter_of(False, i, head) * tile + row for i in range(2)], axis=0)
    half = stat.shape[2] // 2
    attns = []
    for h in range(heads):
        both = jnp.concatenate([send_q[h], mine_q[h]], axis=0)
        scores = jnp.where(col <= token, dot_t(both, keys[...]), -jnp.inf)
        old_top = stat[h, :, :1]
        top = jnp.maximum(old_top, jnp.max(scores, axis=1, keepdims=True))
        expo = jnp.exp(scores - top)
        fade = jnp.exp(old_top - top)
        total = stat[h, :, half : half + 1] * fade + jnp.sum(expo, axis=1, keepdims=True)
        value = acc[h] * fade + dot(expo.astype(BF16), vals[...])
        attns.append((value / total).astype(BF16))
    fetch.wait()
    part = dot(jnp.concatenate(attns, axis=1), weights[...]).astype(BF16)
    send[...] = part[:tile]
    mine[...] = part[tile:]


def attend_kernel(
    table, prefix_len, head_at, send_q, mine_q, w_out, pool, fresh, via_ring, via_both,
    send, mine, keys, vals, sem, *, n_pages, page, kv_heads, group,
):
    head = head_at[0]
    length = prefix_len[0]
    heads, tile, _ = send_q.shape
    kv_of = head * heads // group
    prefix = n_pages * page
    rows = fresh.shape[0]

    copies = old_copies(table, pool, keys, vals, sem, kv_of, kv_heads, n_pages, page)
    for copy in copies:
        copy.start()
    new_copies(
        head, fresh, via_ring, via_both, keys.at[pl.ds(prefix, rows)],
        vals.at[pl.ds(prefix, rows)], sem.at[0, n_pages], sem.at[1, n_pages],
    )
    for copy in copies:
        copy.wait()

    col = lax.broadcasted_iota(jnp.int32, (1, prefix + rows), 1)
    lowest = jnp.where(col < prefix, jnp.where(col < length, -1, rows), col - prefix)
    row = lax.broadcasted_iota(jnp.int32, (tile, 1), 0)
    attns = [[], []]
    for h in range(heads):
        both = jnp.concatenate([send_q[h], mine_q[h]], axis=0)
        token = jnp.concatenate(
            [quarter_of(True, i, head) * tile + row for i in range(2)], axis=0
        )
        scores = jnp.where(lowest <= token, dot_t(both, keys[...]), -jnp.inf)
        top = jnp.max(scores, axis=1, keepdims=True)
        expo = jnp.exp(scores - top)
        total = jnp.sum(expo, axis=1, keepdims=True)
        attns[h] = (dot(expo.astype(BF16), vals[...]) / total).astype(BF16)
    part = dot(jnp.concatenate(attns, axis=1), w_out[...]).astype(BF16)

    send[...] = part[:tile]
    mine[...] = part[tile:]


def quarter_of(own_chip, own_core, head):
    core = head % 2 if own_core else 1 - head % 2
    chip = head // 2 if own_chip else 1 - head // 2
    return chip * 2 + core


def post_kernel(
    head_at, hidden, normed, mine, partner, far, plane, post_gain, left, right, laurel_gain,
    gate, proj, pl_gain, mixed,
):
    total = mine[...].astype(F32) + partner[...].astype(F32) + far[...].astype(F32)
    low = dot_t(normed[...], left[...]).astype(BF16)
    laurel = normed[...].astype(F32) + rms_scale(dot(low, right[...])) * laurel_gain[...]
    state = (hidden[...].astype(F32) + rms_scale(total) * post_gain[...] + laurel) * 2.0 ** (-0.5)
    gated = jax.nn.gelu(dot(state.astype(BF16), gate[...]), approximate=True)
    gated = (gated * plane[...].astype(F32)).astype(BF16)
    mixed[...] = (state + rms_scale(dot(gated, proj[...])) * pl_gain[...]).astype(BF16)


def permute_kernel(owner, spread, after, arranged):
    def place(r, carry):
        arranged[owner[r]] = spread[r]
        return carry

    lax.fori_loop(0, spread.shape[0], place, 0, unroll=8)


def whole(shape):
    zeros = (0,) * len(shape)
    return pl.BlockSpec(shape, lambda *_: zeros)


def on_device(
    hidden_in, layer_input, in_gain, w_query, w_keyval, q_gain, k_gain, w_out, post_gain,
    laurel_left, laurel_right, laurel_gain, w_plgate, w_plproj, pl_gain, kv_pool, page_table,
    prefix_len, decode_owner,
):
    rows, width = hidden_in.shape
    dim = kv_pool.shape[3]
    page = kv_pool.shape[2]
    n_pages = page_table.shape[1]
    kv_heads = kv_pool.shape[1] // 2
    heads = w_query.shape[1] // dim
    prefix = n_pages * page
    total_len = prefix + rows
    blocks = lax.axis_size("blk")
    group = QH // KVH
    n_head = lax.axis_size("head")
    quarter = rows // n_head
    head = lax.axis_index("head").astype(jnp.int32)
    half = dim // 2
    frequency = jnp.asarray((rope_base ** (-np.arange(half) / half))[None], F32)
    scalars = (page_table[0], prefix_len, head[None])

    in_gain, q_gain, k_gain = in_gain[None], q_gain[None], k_gain[None]
    post_gain, laurel_gain, pl_gain = post_gain[None], laurel_gain[None], pl_gain[None]

    tile = rows // 2
    normed, fresh, full_seq, cosine, sine = pl.pallas_call(
        functools.partial(
            prep_kernel, n_pages=n_pages, page=page, kv_heads=kv_heads
        ),
        grid_spec=pltpu.PrefetchScalarGridSpec(
            num_scalar_prefetch=3,
            grid=(rows // tile,),
            in_specs=[
                pl.BlockSpec((tile, width), lambda i, *_: (i, 0)),
                whole((1, width)),
                pl.BlockSpec(memory_space=ANY),
                whole((1, dim)),
                whole((1, half)),
                pl.BlockSpec(memory_space=ANY),
            ],
            out_specs=[
                pl.BlockSpec((tile, width), lambda i, *_: (i, 0)),
                pl.BlockSpec((tile, dim), lambda i, *_: (i, 0)),
                whole((total_len, dim)),
                pl.BlockSpec((tile, half), lambda i, *_: (i, 0)),
                pl.BlockSpec((tile, half), lambda i, *_: (i, 0)),
            ],
            scratch_shapes=[
                pltpu.VMEM((width, dim), BF16),
                pltpu.SemaphoreType.DMA((n_pages + 1,)),
            ],
        ),
        out_shape=[
            jax.ShapeDtypeStruct((rows, width), BF16),
            jax.ShapeDtypeStruct((rows, dim), BF16),
            jax.ShapeDtypeStruct((total_len, dim), BF16),
            jax.ShapeDtypeStruct((rows, half), F32),
            jax.ShapeDtypeStruct((rows, half), F32),
        ],
        name="prep",
    )(*scalars, hidden_in, in_gain, w_keyval, k_gain, frequency, kv_pool)

    def pairs(moves):
        return [(b * n_head + s, b * n_head + t) for b in range(blocks) for s, t in moves]

    via_ring = lax.ppermute(fresh, AXES, pairs(((0, 1), (1, 3), (3, 2), (2, 0))))
    via_both = lax.ppermute(via_ring, AXES, pairs(((0, 1), (3, 2))))
    spread = lax.all_to_all(
        full_seq.reshape(blocks, total_len // blocks, dim), "blk", 0, 0, tiled=True
    )

    queries = pl.pallas_call(
        query_kernel,
        grid=(heads,),
        in_specs=[
            whole((rows, width)),
            pl.BlockSpec((width, dim), lambda i: (0, i)),
            whole((1, dim)),
            whole((rows, half)),
            whole((rows, half)),
        ],
        out_specs=pl.BlockSpec((1, rows, dim), lambda i: (i, 0, 0)),
        out_shape=jax.ShapeDtypeStruct((heads, rows, dim), BF16),
        name="query",
    )(normed, w_query, q_gain, cosine, sine)

    hbm = pl.BlockSpec(memory_space=ANY)
    parts = [jax.ShapeDtypeStruct((quarter, width), BF16)] * 2
    sizes = dict(n_pages=n_pages, page=page, kv_heads=kv_heads, group=group)
    state = (heads, 2 * quarter, dim)

    def query_specs(own_chip):
        return [
            pl.BlockSpec(
                (heads, quarter, dim),
                lambda i, *m, core=core: (0, quarter_of(own_chip, core, m[-1][0]), 0),
            )
            for core in (False, True)
        ]

    acc, stat = pl.pallas_call(
        functools.partial(attend_old_kernel, **sizes),
        grid_spec=pltpu.PrefetchScalarGridSpec(
            num_scalar_prefetch=3,
            grid=(1,),
            in_specs=query_specs(False) + [hbm],
            out_specs=[whole(state)] * 2,
            scratch_shapes=[
                pltpu.VMEM((prefix, dim), BF16),
                pltpu.VMEM((prefix, dim), BF16),
                pltpu.SemaphoreType.DMA((2, n_pages)),
            ],
        ),
        out_shape=[jax.ShapeDtypeStruct(state, F32)] * 2,
        name="attend_old",
    )(*scalars, queries, queries, kv_pool)

    send, mine = pl.pallas_call(
        attend_new_kernel,
        grid_spec=pltpu.PrefetchScalarGridSpec(
            num_scalar_prefetch=1,
            grid=(1,),
            in_specs=query_specs(False)
            + [whole(state), whole(state)]
            + [hbm] * 4,
            out_specs=[whole((quarter, width))] * 2,
            scratch_shapes=[
                pltpu.VMEM((rows, dim), BF16),
                pltpu.VMEM((rows, dim), BF16),
                pltpu.VMEM(w_out.shape, BF16),
                pltpu.SemaphoreType.DMA((3,)),
            ],
        ),
        out_shape=parts,
        name="attend_new",
    )(scalars[2], queries, queries, acc, stat, w_out, fresh, via_ring, via_both)

    core_pairs = pairs(((0, 1), (1, 0), (2, 3), (3, 2)))
    chip_pairs = pairs(((0, 2), (1, 3), (2, 0), (3, 1)))
    partner = lax.ppermute(send, AXES, core_pairs)
    pair_sum = (mine.astype(F32) + partner.astype(F32)).astype(BF16)
    far = lax.ppermute(pair_sum, AXES, chip_pairs)
    send, mine = pl.pallas_call(
        functools.partial(attend_kernel, **sizes),
        grid_spec=pltpu.PrefetchScalarGridSpec(
            num_scalar_prefetch=3,
            grid=(1,),
            in_specs=query_specs(True) + [whole(w_out.shape)] + [hbm] * 4,
            out_specs=[whole((quarter, width))] * 2,
            scratch_shapes=[
                pltpu.VMEM((total_len, dim), BF16),
                pltpu.VMEM((total_len, dim), BF16),
                pltpu.SemaphoreType.DMA((2, n_pages + 1)),
            ],
        ),
        out_shape=parts,
        name="attend_own",
    )(*scalars, queries, queries, w_out, kv_pool, fresh, via_ring, via_both)
    partner = lax.ppermute(send, AXES, core_pairs)

    mixed = pl.pallas_call(
        post_kernel,
        grid_spec=pltpu.PrefetchScalarGridSpec(
            num_scalar_prefetch=1,
            grid=(1,),
            in_specs=[
                pl.BlockSpec((quarter, width), lambda i, h: (h[0], 0)),
                pl.BlockSpec((quarter, width), lambda i, h: (h[0], 0)),
                whole((quarter, width)),
                whole((quarter, width)),
                whole((quarter, width)),
                whole(layer_input.shape),
                whole((1, width)),
                whole(laurel_left.shape[::-1]),
                whole(laurel_right.shape),
                whole((1, width)),
                whole(w_plgate.shape),
                whole(w_plproj.shape),
                whole((1, width)),
            ],
            out_specs=whole((quarter, width)),
        ),
        out_shape=jax.ShapeDtypeStruct((quarter, width), BF16),
        name="post",
    )(
        scalars[2], hidden_in, normed, mine, partner, far, layer_input, post_gain, laurel_left.T,
        laurel_right, laurel_gain, w_plgate, w_plproj, pl_gain,
    )

    arranged = pl.pallas_call(
        permute_kernel,
        grid_spec=pltpu.PrefetchScalarGridSpec(
            num_scalar_prefetch=1,
            grid=(1,),
            in_specs=[whole(spread.shape), pl.BlockSpec(memory_space=ANY)],
            out_specs=whole(spread.shape),
        ),
        out_shape=jax.ShapeDtypeStruct(spread.shape, spread.dtype),
        name="permute",
    )(decode_owner, spread, pair_sum)
    owned = lax.all_to_all(arranged, "blk", 0, 0, tiled=True)
    return mixed, owned.reshape(1, 1, total_len, dim)


def solution(mesh):
    in_specs = (
        P("blk", None),
        P(("blk", "head"), None),
        P(),
        P(None, "head"),
        P(None, "head"),
        P(),
        P(),
        P("head", None),
        P(),
        P(),
        P(),
        P(),
        P(),
        P(),
        P(),
        P("blk", None, None, None),
        P("blk", None),
        P("blk"),
        P(),
    )
    out_specs = (P(("blk", "head"), None), P("head", "blk", None, None))
    return jax.shard_map(
        on_device, mesh=mesh, in_specs=in_specs, out_specs=out_specs, check_vma=False
    )
```
